32 devices in a mesh: groups: 2 (over y), shot: 4 (over z), rcv: 2 (over x), rep: 2 (over core).
Axes of the slice: x: 2, y: 2, z: 4, core: 2. Of those that a mesh axis runs over, the one named last changes fastest.
Arguments:
- records: float32 [64, 131072], P(('groups', 'rcv'), ('shot', 'rep')), parts along dimension 0, may hold values from -6 to 6
- offsets: int32 [16, 32], P(('groups', 'shot', 'rep')), parts along dimension 0, may hold values from 0 to 130560, as said below
- filter_index: int32 [16, 32], P(('groups', 'shot', 'rep')), parts along dimension 0, may hold values from 0 to 7
- signatures: bfloat16 [8, 128], replicated, may hold values from -0.5 to 0.5
- thresholds: float32 [2, 256], replicated, may hold values from 0.3 to 2
Outputs:
- model_field: float32 [16, 32, 32, 512], P(('groups', 'shot', 'rep'), 'rcv'), parts along dimension 0
- residual: float32 [64, 131072], P(('groups', 'rcv'), ('shot', 'rep')), parts along dimension 0
The draws below stay inside these ranges and needn't reach their ends.
There are 2 independent parts, one for each index of `groups`. The reference program is written for one: setup_inputs(seed, part) draws one part's arguments, and reference() takes and returns one part's arrays. A program takes and returns all parts, laid end to end along the dimension named above; an argument that names none is the same for every part. Nothing has to cross between parts.
Inputs may be any that keep to these rules, and one draw needn't show every extreme that they name: Every offset is a multiple of 128. Shot (x,y) starts in slab offsets[x,y] // 16384; within one row x of the shot grid at most 8 shots start in any one slab, and this bound is reached in every row. Every shot ends inside the record.
All inputs are finite; a program needn't handle non-finite values.
Results may differ from the reference program's by a relative error of at most 0.024.
Values may be sent and summed in bfloat16 or wider, within the bound.
A program may use at most 64 MiB of HBM per device.

```python
import math
import jax
import jax.numpy as jnp
from jax import lax

NR = 32
SY = 32
NT = 512
BLOCK = 128
NSIG = 8
ITERS = 2
SLABB = 128
NSLAB = 8
SX = 8
CAP = 8
L = 131072
FB = 256


def draw_offsets(key, part):
    hot_owners = jax.random.permutation(jax.random.fold_in(key, 101), NSLAB)[:2]
    slot_owner = jnp.arange(NSLAB * CAP, dtype=jnp.int32) // CAP
    is_hot = jnp.any(slot_owner[:, None] == hot_owners[None, :], axis=1)

    def one_row(row_number):
        row_key = jax.random.fold_in(key, row_number)
        scores = jax.random.permutation(jax.random.fold_in(row_key, 1), NSLAB * CAP)
        scores = scores + jnp.where(is_hot, 0, NSLAB * CAP)
        chosen = slot_owner[jnp.argsort(scores)[:SY]]
        owners = chosen[jax.random.permutation(jax.random.fold_in(row_key, 2), SY)]
        within = jax.random.randint(jax.random.fold_in(row_key, 3), (SY,), 0, SLABB)
        within = jnp.where(owners == NSLAB - 1, within % (SLABB - NT // BLOCK + 1), within)
        return ((owners * SLABB + within) * BLOCK).astype(jnp.int32)
    return jax.vmap(one_row)(jnp.arange(SX))


def set_ends(drawn, stream_key, least, largest):
    index_at = [jax.random.randint(jax.random.fold_in(stream_key, axis), (), 0, length) for axis, length in enumerate(drawn.shape)]
    widest = drawn.shape.index(max(drawn.shape))
    neighbour = index_at[:widest] + [(index_at[widest] + 1) % drawn.shape[widest]] + index_at[widest + 1:]
    return drawn.at[tuple(index_at)].set(least).at[tuple(neighbour)].set(largest)


def level_of(own_key, dims, cuts, smallest, largest):
    def one(dim, parts):
        steps = jax.random.uniform(jax.random.fold_in(jax.random.fold_in(own_key, 6), dim), (parts,), jnp.float32, smallest / len(cuts), largest / len(cuts))
        return jnp.repeat(jnp.exp(steps), dims[dim] // parts).reshape((-1,) + (1,) * (len(dims) - dim - 1))

    factor_of = one(*cuts[0])
    for cut in cuts[1:]:
        factor_of = factor_of * one(*cut)
    return factor_of


def gaussian(own_key, extent, scale, bound, cuts=(), held_as=jnp.bfloat16):
    entries = scale * jax.random.normal(own_key, extent, jnp.float32)
    if cuts:
        entries = entries * level_of(own_key, extent, cuts, -0.22, 0.18)
    return jnp.clip(entries, -bound, bound).astype(held_as)


def setup_inputs(seed: int = 0, part: int = 0) -> dict:
    key_of = jax.random.split(jax.random.key(seed), 6)
    part_splits = jax.random.split(jax.random.fold_in(key_of[5], part), 6)
    return {
        "records": gaussian(part_splits[0], (NR, L), 1.0, 6.0, ((0, 2), (1, 8)), jnp.float32),
        "offsets": draw_offsets(jax.random.fold_in(jax.random.fold_in(key_of[5], part), 71), part),
        "filter_index": set_ends(jax.random.randint(part_splits[2], (SX, SY), 0, NSIG), jax.random.fold_in(part_splits[2], 1), 0, NSIG - 1).astype(jnp.int32),
        "signatures": gaussian(key_of[3], (NSIG, BLOCK), BLOCK ** -0.5, 0.5),
        "thresholds": jnp.clip(jnp.exp(jax.random.uniform(key_of[4], (ITERS, FB), jnp.float32, math.log(0.3), math.log(2.0))), 0.3, 2.0),
    }


def time_table(count):
    samples = jnp.arange(count)
    bin_index = jnp.arange(count // 2)[:, None]
    angles = 2.0 * math.pi / count * (bin_index * samples[None, :] % count).astype(jnp.float32)
    parity = jnp.where(samples % 2 == 0, 1.0, -1.0).astype(jnp.float32)
    cosine = jnp.where(bin_index == 0, math.sqrt(1.0 / count), math.sqrt(2.0 / count)) * jnp.cos(angles)
    sine_part = jnp.where(bin_index == 0, math.sqrt(1.0 / count) * parity[None, :], -math.sqrt(2.0 / count) * jnp.sin(angles))
    return jnp.stack([cosine, sine_part]).astype(jnp.bfloat16)

def shot_table(count):
    positions = jnp.arange(count)
    angles = 2.0 * math.pi / count * (positions[:, None] * positions[None, :] % count).astype(jnp.float32)
    scaling = 1.0 / math.sqrt(count)
    cosine = scaling * jnp.cos(angles)
    sine_part = scaling * jnp.sin(angles)
    upper_half = jnp.stack([cosine, sine_part], axis=1)
    lower_half = jnp.stack([-sine_part, cosine], axis=1)
    return jnp.stack([upper_half, lower_half]).astype(jnp.bfloat16)

def toeplitz_pair(shot_taps):
    tap_count = shot_taps.shape[1]
    row_index = jnp.arange(tap_count)[:, None]
    col_index = jnp.arange(tap_count)[None, :]
    full_table = shot_taps[:, (row_index - col_index) % tap_count]
    zero_table = jnp.zeros_like(full_table)
    return (jnp.where(row_index >= col_index, full_table, zero_table), jnp.where(row_index < col_index, full_table, zero_table))

def rounded(values):
    return lax.optimization_barrier(values.astype(jnp.bfloat16)).astype(jnp.float32)

def filter_forward(traces, shot_taps):
    lower_part, upper_part = toeplitz_pair(shot_taps)
    tap_count = shot_taps.shape[1]
    blocks = traces.reshape(traces.shape[0], traces.shape[1], -1, tap_count).astype(jnp.float32)
    earlier = jnp.concatenate([jnp.zeros_like(blocks[:, :, :1]), blocks[:, :, :-1]], axis=2)
    high = lax.Precision.HIGHEST
    result = jnp.einsum('spq,rsbq->rsbp', lower_part.astype(jnp.float32), blocks, precision=high)
    result = result + jnp.einsum('spq,rsbq->rsbp', upper_part.astype(jnp.float32), earlier, precision=high)
    return result.reshape(traces.shape)

def filter_adjoint(traces, shot_taps):
    lower_part, upper_part = toeplitz_pair(shot_taps)
    tap_count = shot_taps.shape[1]
    blocks = traces.reshape(traces.shape[0], traces.shape[1], -1, tap_count).astype(jnp.float32)
    later_blocks = jnp.concatenate([blocks[:, :, 1:], jnp.zeros_like(blocks[:, :, :1])], axis=2)
    high = lax.Precision.HIGHEST
    result = jnp.einsum('spq,rsbp->rsbq', lower_part.astype(jnp.float32), blocks, precision=high)
    result = result + jnp.einsum('spq,rsbp->rsbq', upper_part.astype(jnp.float32), later_blocks, precision=high)
    return result.reshape(traces.shape)

def reference(records, offsets, filter_index, signatures, thresholds):
    high = lax.Precision.HIGHEST
    shot_taps = signatures[filter_index]
    sample_range = jnp.arange(NT, dtype=jnp.int32)
    table_time = time_table(NT).astype(jnp.float32)
    table_x = shot_table(SX).astype(jnp.float32)
    table_y = shot_table(SY).astype(jnp.float32)
    table_r = shot_table(NR).astype(jnp.float32)

    def correlate(record_field):
        record_low = record_field.astype(jnp.bfloat16)

        def one_row(inputs):
            row_offsets, row_taps = inputs
            window = record_low[:, row_offsets[:, None] + sample_range[None, :]]
            return filter_adjoint(window, row_taps)
        return lax.map(one_row, (offsets, shot_taps))

    def blend(field_data):
        field_low = field_data.astype(jnp.bfloat16)

        def one_row(record_total, inputs):
            row_field, row_offsets, row_taps = inputs
            shots = rounded(filter_forward(row_field, row_taps))
            record_total = record_total.at[:, row_offsets[:, None] + sample_range[None, :]].add(shots)
            return (record_total, None)
        record_total, _ = lax.scan(one_row, jnp.zeros((NR, L), jnp.float32), (field_low, offsets, shot_taps))
        return record_total

    def shrink(field_data, level_index):
        section_data = rounded(jnp.einsum('ckt,xryt->ckxry', table_time, rounded(field_data), precision=high))
        section_data = rounded(jnp.einsum('akbx,bfxry->afkry', table_x, section_data, precision=high))
        section_data = rounded(jnp.einsum('ajby,bfkry->afkrj', table_y, section_data, precision=high))
        coefficients = jnp.einsum('aqbr,bfkrj->afkqj', table_r, section_data, precision=high)
        magnitude = jnp.sqrt(coefficients[0] * coefficients[0] + coefficients[1] * coefficients[1])
        threshold_row = thresholds[level_index][:, None, None, None]
        factor = 1.0 - threshold_row / jnp.maximum(magnitude, threshold_row)
        section_data = rounded(coefficients * factor[None])
        section_data = rounded(jnp.einsum('aqbr,afkqj->bfkrj', table_r, section_data, precision=high))
        section_data = rounded(jnp.einsum('ajby,afkrj->bfkry', table_y, section_data, precision=high))
        section_data = rounded(jnp.einsum('akbx,afkry->bfxry', table_x, section_data, precision=high))
        return jnp.einsum('ckt,ckxry->xryt', table_time, section_data, precision=high)
    model_field = shrink(correlate(records), 0)
    residual = records
    for level_index in range(1, ITERS):
        residual = records - blend(model_field)
        model_field = shrink(model_field + correlate(residual), level_index)
    return (model_field, residual)
```

```python
import math

import jax
import jax.numpy as jnp
from jax import lax
from jax.experimental import pallas as pl
from jax.experimental.pallas import tpu as pltpu
from jax.sharding import PartitionSpec as P

NT = 512


def from_behind(value, axis, steps):
    count = lax.axis_size(axis)
    first, last = (max(0, -steps), min(count, count - steps))
    return lax.ppermute(value, axis, [(source, source + steps) for source in range(first, last)])


def time_table(count):
    samples = jnp.arange(count)
    bin_index = jnp.arange(count // 2)[:, None]
    angles = 2.0 * math.pi / count * (bin_index * samples[None, :] % count).astype(jnp.float32)
    parity = jnp.where(samples % 2 == 0, 1.0, -1.0).astype(jnp.float32)
    cosine = jnp.where(bin_index == 0, math.sqrt(1.0 / count), math.sqrt(2.0 / count)) * jnp.cos(
        angles
    )
    sine_part = jnp.where(
        bin_index == 0,
        math.sqrt(1.0 / count) * parity[None, :],
        -math.sqrt(2.0 / count) * jnp.sin(angles),
    )
    return jnp.stack([cosine, sine_part]).astype(jnp.bfloat16)


def shot_table(count):
    positions = jnp.arange(count)
    angles = (
        2.0
        * math.pi
        / count
        * (positions[:, None] * positions[None, :] % count).astype(jnp.float32)
    )
    scaling = 1.0 / math.sqrt(count)
    cosine = scaling * jnp.cos(angles)
    sine_part = scaling * jnp.sin(angles)
    upper_half = jnp.stack([cosine, sine_part], axis=1)
    lower_half = jnp.stack([-sine_part, cosine], axis=1)
    return jnp.stack([upper_half, lower_half]).astype(jnp.bfloat16)


def toeplitz_kernel(taps_ref, forward_ref, adjoint_ref):
    tap_count = taps_ref.shape[1]
    row_index = lax.broadcasted_iota(jnp.int32, (tap_count, tap_count), 0)
    col_index = lax.broadcasted_iota(jnp.int32, (tap_count, tap_count), 1)
    for index in range(taps_ref.shape[0]):
        row = jnp.broadcast_to(taps_ref[index : index + 1, :], (tap_count, tap_count))
        turned = pltpu.roll(row, 0, 1, stride=1, stride_axis=0)
        zeros = jnp.zeros_like(turned)
        near = jnp.where(col_index >= row_index, turned, zeros)
        far = jnp.where(col_index < row_index, turned, zeros)
        forward_ref[index, :tap_count, :] = near.astype(jnp.bfloat16)
        forward_ref[index, tap_count:, :] = far.astype(jnp.bfloat16)
        adjoint_ref[index, :tap_count, :] = near.T.astype(jnp.bfloat16)
        adjoint_ref[index, tap_count:, :] = far.T.astype(jnp.bfloat16)


def toeplitz_tables(signatures):
    count, tap_count = signatures.shape
    shape = jax.ShapeDtypeStruct((count, 2 * tap_count, tap_count), jnp.bfloat16)
    return pl.pallas_call(
        toeplitz_kernel,
        out_shape=(shape, shape),
        in_specs=[pl.BlockSpec(memory_space=pltpu.VMEM)],
        out_specs=(pl.BlockSpec(memory_space=pltpu.VMEM),) * 2,
    )(signatures.astype(jnp.float32))


def apply_filter(traces, table, adjoint):
    empty = jnp.zeros_like(traces[:, :1])
    if adjoint:
        other = jnp.concatenate([traces[:, 1:], empty], axis=1)
    else:
        other = jnp.concatenate([empty, traces[:, :-1]], axis=1)
    return jnp.einsum(
        "sbrp,spq->sbrq",
        jnp.concatenate([traces, other], axis=3),
        table,
        preferred_element_type=jnp.float32,
    )


def rank_in_row(owners):
    shot_count = owners.shape[1]
    same_owner = owners[:, :, None] == owners[:, None, :]
    earlier = jnp.arange(shot_count)[None, :] < jnp.arange(shot_count)[:, None]
    return jnp.sum(same_owner & earlier[None], axis=2)


def to_slabs(payload):
    return lax.all_to_all(payload, ("shot", "rep"), split_axis=0, concat_axis=0, tiled=True)


def to_shots(payload):
    return lax.all_to_all(payload, ("shot", "rep"), split_axis=0, concat_axis=0, tiled=True)


def soft_limit(coefficients, threshold_row):
    magnitude = jnp.sqrt(coefficients[0] * coefficients[0] + coefficients[1] * coefficients[1])
    threshold_view = threshold_row[None, :, None, None]
    factor = 1.0 - threshold_view / jnp.maximum(magnitude, threshold_view)
    return (coefficients * factor[None]).astype(jnp.bfloat16)


def shrink(field_data, threshold_row, tables):
    table_time, table_x, table_y, table_r = tables
    rows_here, local_rcv, shot_count, sample_count = field_data.shape
    spectrum = jnp.einsum(
        "ckt,xryt->xckry",
        table_time,
        field_data.astype(jnp.bfloat16),
        preferred_element_type=jnp.float32,
    ).astype(jnp.bfloat16)
    bin_count = spectrum.shape[2]
    spectrum = spectrum.reshape(rows_here, 2, bin_count, local_rcv * shot_count)
    section_data = jnp.einsum(
        "akbx,xbfz->akfz",
        table_x,
        lax.all_to_all(spectrum, ("shot", "rep"), split_axis=2, concat_axis=0, tiled=True),
        preferred_element_type=jnp.float32,
    ).astype(jnp.bfloat16)
    all_rows, row_bins = (section_data.shape[1], section_data.shape[2])
    section_data = section_data.reshape(2, all_rows, row_bins, local_rcv, shot_count)
    section_data = lax.all_to_all(section_data, "rcv", split_axis=2, concat_axis=3, tiled=True)
    section_data = jnp.einsum(
        "ajby,bkfry->akfrj", table_y, section_data, preferred_element_type=jnp.float32
    ).astype(jnp.bfloat16)
    coefficients = jnp.einsum(
        "aqbr,bkfrj->akfqj", table_r, section_data, preferred_element_type=jnp.float32
    )
    shrunk = soft_limit(coefficients, threshold_row)
    section_data = jnp.einsum(
        "aqbr,akfqj->bkfrj", table_r, shrunk, preferred_element_type=jnp.float32
    ).astype(jnp.bfloat16)
    section_data = jnp.einsum(
        "ajby,akfrj->bkfry", table_y, section_data, preferred_element_type=jnp.float32
    ).astype(jnp.bfloat16)
    section_data = lax.all_to_all(section_data, "rcv", split_axis=3, concat_axis=2, tiled=True)
    section_data = section_data.reshape(2, all_rows, row_bins, local_rcv * shot_count)
    section_data = jnp.einsum(
        "akbx,akfz->bxfz", table_x, section_data, preferred_element_type=jnp.float32
    ).astype(jnp.bfloat16)
    result = jnp.einsum(
        "ckt,cxkz->xzt",
        table_time,
        lax.all_to_all(section_data, ("shot", "rep"), split_axis=1, concat_axis=2, tiled=True),
        preferred_element_type=jnp.float32,
    )
    return result.reshape(rows_here, local_rcv, shot_count, sample_count)


def body(records, offsets, filter_index, signatures, thresholds):
    rows_here, shot_count = offsets.shape
    local_rcv, slab_len = records.shape
    slab_count = lax.axis_size(("shot", "rep"))
    rcv_count = lax.axis_size("rcv")
    tap_count = signatures.shape[1]
    sample_count = NT
    slab_blocks = slab_len // tap_count
    trace_blocks = sample_count // tap_count
    capacity = max(2, 2 * shot_count // slab_count)
    slot_count = slab_count * rows_here * capacity
    forward_tables, adjoint_tables = toeplitz_tables(signatures)
    flat_index = filter_index.reshape(-1)
    forward_table = forward_tables[flat_index]
    adjoint_table = adjoint_tables[flat_index]
    owners = offsets // slab_len
    row_ids = jnp.arange(rows_here, dtype=jnp.int32)[:, None]
    slot_index = (
        owners * (rows_here * capacity) + row_ids * capacity + rank_in_row(owners)
    ).reshape(-1)
    every_offset = lax.all_gather(offsets, ("shot", "rep"), axis=0, tiled=True)
    every_owner = every_offset // slab_len
    every_start = every_offset // tap_count % slab_blocks
    every_rank = rank_in_row(every_owner)
    mine_mask = every_owner == lax.axis_index(("shot", "rep"))
    levels = jnp.arange(capacity, dtype=jnp.int32)
    picked = mine_mask[:, :, None] & (every_rank[:, :, None] == levels[None, None, :])
    table_in = jnp.sum(jnp.where(picked, every_start[:, :, None] + 1, 0), axis=1).reshape(-1)
    filled = table_in > 0
    block_steps = jnp.arange(trace_blocks, dtype=jnp.int32)
    target = jnp.where(
        filled[:, None],
        table_in[:, None] - 1 + block_steps[None, :],
        slab_blocks + trace_blocks - 1,
    )

    def correlate(record_field):
        record_low = (
            record_field.astype(jnp.bfloat16)
            .reshape(local_rcv, slab_blocks, tap_count)
            .transpose(1, 0, 2)
        )
        rim_blocks = from_behind(record_low[: trace_blocks - 1], ("shot", "rep"), -1)
        extended = jnp.concatenate(
            [record_low, rim_blocks, jnp.zeros((1, local_rcv, tap_count), jnp.bfloat16)], axis=0
        )
        windows = extended[target.reshape(-1)].reshape(
            slot_count, trace_blocks, local_rcv, tap_count
        )
        returned = to_shots(windows)
        traces = returned[slot_index]
        terms = apply_filter(traces, adjoint_table, True)
        terms = terms.reshape(rows_here, shot_count, trace_blocks, local_rcv, tap_count).transpose(
            0, 3, 1, 2, 4
        )
        return terms.reshape(rows_here, local_rcv, shot_count, sample_count)

    tables = (
        time_table(sample_count),
        shot_table(slab_count * rows_here),
        shot_table(shot_count),
        shot_table(local_rcv * rcv_count),
    )
    row_bins = sample_count // 2 // slab_count
    rcv_bins = row_bins // rcv_count
    bin_start = lax.axis_index(("shot", "rep")) * row_bins + lax.axis_index("rcv") * rcv_bins

    def threshold_for(level_index):
        return lax.dynamic_slice_in_dim(thresholds[level_index], bin_start, rcv_bins)

    model_field = shrink(correlate(records), threshold_for(0), tables)
    level_index = 1
    traces = model_field.astype(jnp.bfloat16).reshape(
        rows_here, local_rcv, shot_count, trace_blocks, tap_count
    )
    traces = traces.transpose(0, 2, 3, 1, 4).reshape(
        rows_here * shot_count, trace_blocks, local_rcv, tap_count
    )
    shots = apply_filter(traces, forward_table, False).astype(jnp.bfloat16)
    outgoing = (
        jnp.zeros((slot_count, trace_blocks, local_rcv, tap_count), jnp.bfloat16)
        .at[slot_index]
        .set(shots)
    )
    arrived = to_slabs(outgoing)
    slab_total = jnp.zeros((slab_blocks + trace_blocks, local_rcv, tap_count), jnp.float32)
    for block_step in range(trace_blocks):
        slab_total = slab_total.at[target[:, block_step]].add(
            arrived[:, block_step].astype(jnp.float32)
        )
    spill_over = slab_total[slab_blocks : slab_blocks + trace_blocks - 1]
    carried = from_behind(spill_over, ("shot", "rep"), 1)
    blended = slab_total[:slab_blocks].at[: trace_blocks - 1].add(carried)
    residual = records - blended.transpose(1, 0, 2).reshape(local_rcv, slab_len)
    model_field = shrink(model_field + correlate(residual), threshold_for(level_index), tables)
    return (model_field, residual)


def solution(mesh):
    in_specs = (
        P(("groups", "rcv"), ("shot", "rep")),
        P(("groups", "shot", "rep"), None),
        P(("groups", "shot", "rep"), None),
        P(),
        P(),
    )
    out_specs = (
        P(("groups", "shot", "rep"), "rcv", None, None),
        P(("groups", "rcv"), ("shot", "rep")),
    )
    return jax.shard_map(body, mesh=mesh, in_specs=in_specs, out_specs=out_specs, check_vma=False)
```

```python
import functools
import math

import jax
import jax.numpy as jnp
import numpy as np
from jax import lax
from jax.experimental import pallas as pl
from jax.experimental.pallas import tpu as pltpu
from jax.sharding import PartitionSpec as P

NT = 512


def from_behind(value, axis, steps):
    count = lax.axis_size(axis)
    first, last = (max(0, -steps), min(count, count - steps))
    return lax.ppermute(value, axis, [(source, source + steps) for source in range(first, last)])


def time_table(count):
    samples = jnp.arange(count)
    bin_index = jnp.arange(count // 2)[:, None]
    angles = 2.0 * math.pi / count * (bin_index * samples[None, :] % count).astype(jnp.float32)
    parity = jnp.where(samples % 2 == 0, 1.0, -1.0).astype(jnp.float32)
    cosine = jnp.where(bin_index == 0, math.sqrt(1.0 / count), math.sqrt(2.0 / count)) * jnp.cos(
        angles
    )
    sine_part = jnp.where(
        bin_index == 0,
        math.sqrt(1.0 / count) * parity[None, :],
        -math.sqrt(2.0 / count) * jnp.sin(angles),
    )
    return jnp.stack([cosine, sine_part]).astype(jnp.bfloat16)


def shot_table(count):
    positions = jnp.arange(count)
    angles = (
        2.0
        * math.pi
        / count
        * (positions[:, None] * positions[None, :] % count).astype(jnp.float32)
    )
    scaling = 1.0 / math.sqrt(count)
    cosine = scaling * jnp.cos(angles)
    sine_part = scaling * jnp.sin(angles)
    upper_half = jnp.stack([cosine, sine_part], axis=1)
    lower_half = jnp.stack([-sine_part, cosine], axis=1)
    return jnp.stack([upper_half, lower_half]).astype(jnp.bfloat16)


def toeplitz_kernel(taps_ref, forward_ref, adjoint_ref):
    tap_count = taps_ref.shape[1]
    row_index = lax.broadcasted_iota(jnp.int32, (tap_count, tap_count), 0)
    col_index = lax.broadcasted_iota(jnp.int32, (tap_count, tap_count), 1)
    for index in range(taps_ref.shape[0]):
        row = jnp.broadcast_to(taps_ref[index : index + 1, :], (tap_count, tap_count))
        turned = pltpu.roll(row, 0, 1, stride=1, stride_axis=0)
        zeros = jnp.zeros_like(turned)
        near = jnp.where(col_index >= row_index, turned, zeros)
        far = jnp.where(col_index < row_index, turned, zeros)
        forward_ref[index, :tap_count, :] = near.astype(jnp.bfloat16)
        forward_ref[index, tap_count:, :] = far.astype(jnp.bfloat16)
        adjoint_ref[index, :tap_count, :] = near.T.astype(jnp.bfloat16)
        adjoint_ref[index, tap_count:, :] = far.T.astype(jnp.bfloat16)


def toeplitz_tables(signatures):
    count, tap_count = signatures.shape
    shape = jax.ShapeDtypeStruct((count, 2 * tap_count, tap_count), jnp.bfloat16)
    return pl.pallas_call(
        toeplitz_kernel,
        out_shape=(shape, shape),
        in_specs=[pl.BlockSpec(memory_space=pltpu.VMEM)],
        out_specs=(pl.BlockSpec(memory_space=pltpu.VMEM),) * 2,
    )(signatures.astype(jnp.float32))


def apply_filter(traces, table, adjoint):
    empty = jnp.zeros_like(traces[:, :1])
    if adjoint:
        other = jnp.concatenate([traces[:, 1:], empty], axis=1)
    else:
        other = jnp.concatenate([empty, traces[:, :-1]], axis=1)
    return jnp.einsum(
        "sbrp,spq->sbrq",
        jnp.concatenate([traces, other], axis=3),
        table,
        preferred_element_type=jnp.float32,
    )


def rank_in_row(owners):
    shot_count = owners.shape[1]
    same_owner = owners[:, :, None] == owners[:, None, :]
    earlier = jnp.arange(shot_count)[None, :] < jnp.arange(shot_count)[:, None]
    return jnp.sum(same_owner & earlier[None], axis=2)


def to_slabs(payload):
    return lax.all_to_all(payload, ("shot", "rep"), split_axis=0, concat_axis=0, tiled=True)


def to_shots(payload):
    return lax.all_to_all(payload, ("shot", "rep"), split_axis=0, concat_axis=0, tiled=True)


def soft_limit(coefficients, threshold_row):
    magnitude = jnp.sqrt(coefficients[0] * coefficients[0] + coefficients[1] * coefficients[1])
    threshold_view = threshold_row[None, :, None, None]
    factor = 1.0 - threshold_view / jnp.maximum(magnitude, threshold_view)
    return (coefficients * factor[None]).astype(jnp.bfloat16)


def shrink(field_data, threshold_row, tables):
    table_time, table_x, table_y, table_r = tables
    rows_here, local_rcv, shot_count, sample_count = field_data.shape
    spectrum = jnp.einsum(
        "ckt,xryt->xckry",
        table_time,
        field_data.astype(jnp.bfloat16),
        preferred_element_type=jnp.float32,
    ).astype(jnp.bfloat16)
    bin_count = spectrum.shape[2]
    spectrum = spectrum.reshape(rows_here, 2, bin_count, local_rcv * shot_count)
    section_data = jnp.einsum(
        "akbx,xbfz->akfz",
        table_x,
        lax.all_to_all(spectrum, ("shot", "rep"), split_axis=2, concat_axis=0, tiled=True),
        preferred_element_type=jnp.float32,
    ).astype(jnp.bfloat16)
    all_rows, row_bins = (section_data.shape[1], section_data.shape[2])
    section_data = section_data.reshape(2, all_rows, row_bins, local_rcv, shot_count)
    section_data = lax.all_to_all(section_data, "rcv", split_axis=2, concat_axis=3, tiled=True)
    section_data = jnp.einsum(
        "ajby,bkfry->akfrj", table_y, section_data, preferred_element_type=jnp.float32
    ).astype(jnp.bfloat16)
    coefficients = jnp.einsum(
        "aqbr,bkfrj->akfqj", table_r, section_data, preferred_element_type=jnp.float32
    )
    shrunk = soft_limit(coefficients, threshold_row)
    section_data = jnp.einsum(
        "aqbr,akfqj->bkfrj", table_r, shrunk, preferred_element_type=jnp.float32
    ).astype(jnp.bfloat16)
    section_data = jnp.einsum(
        "ajby,akfrj->bkfry", table_y, section_data, preferred_element_type=jnp.float32
    ).astype(jnp.bfloat16)
    section_data = lax.all_to_all(section_data, "rcv", split_axis=3, concat_axis=2, tiled=True)
    section_data = section_data.reshape(2, all_rows, row_bins, local_rcv * shot_count)
    section_data = jnp.einsum(
        "akbx,akfz->bxfz", table_x, section_data, preferred_element_type=jnp.float32
    ).astype(jnp.bfloat16)
    result = jnp.einsum(
        "ckt,cxkz->xzt",
        table_time,
        lax.all_to_all(section_data, ("shot", "rep"), split_axis=1, concat_axis=2, tiled=True),
        preferred_element_type=jnp.float32,
    )
    return result.reshape(rows_here, local_rcv, shot_count, sample_count)


def body_by_rows(records, offsets, filter_index, signatures, thresholds):
    rows_here, shot_count = offsets.shape
    local_rcv, slab_len = records.shape
    slab_count = lax.axis_size(("shot", "rep"))
    rcv_count = lax.axis_size("rcv")
    tap_count = signatures.shape[1]
    sample_count = NT
    slab_blocks = slab_len // tap_count
    trace_blocks = sample_count // tap_count
    capacity = max(2, 2 * shot_count // slab_count)
    slot_count = slab_count * rows_here * capacity
    forward_tables, adjoint_tables = toeplitz_tables(signatures)
    flat_index = filter_index.reshape(-1)
    forward_table = forward_tables[flat_index]
    adjoint_table = adjoint_tables[flat_index]
    owners = offsets // slab_len
    row_ids = jnp.arange(rows_here, dtype=jnp.int32)[:, None]
    slot_index = (
        owners * (rows_here * capacity) + row_ids * capacity + rank_in_row(owners)
    ).reshape(-1)
    every_offset = lax.all_gather(offsets, ("shot", "rep"), axis=0, tiled=True)
    every_owner = every_offset // slab_len
    every_start = every_offset // tap_count % slab_blocks
    every_rank = rank_in_row(every_owner)
    mine_mask = every_owner == lax.axis_index(("shot", "rep"))
    levels = jnp.arange(capacity, dtype=jnp.int32)
    picked = mine_mask[:, :, None] & (every_rank[:, :, None] == levels[None, None, :])
    table_in = jnp.sum(jnp.where(picked, every_start[:, :, None] + 1, 0), axis=1).reshape(-1)
    filled = table_in > 0
    block_steps = jnp.arange(trace_blocks, dtype=jnp.int32)
    target = jnp.where(
        filled[:, None],
        table_in[:, None] - 1 + block_steps[None, :],
        slab_blocks + trace_blocks - 1,
    )

    def correlate(record_field):
        record_low = (
            record_field.astype(jnp.bfloat16)
            .reshape(local_rcv, slab_blocks, tap_count)
            .transpose(1, 0, 2)
        )
        rim_blocks = from_behind(record_low[: trace_blocks - 1], ("shot", "rep"), -1)
        extended = jnp.concatenate(
            [record_low, rim_blocks, jnp.zeros((1, local_rcv, tap_count), jnp.bfloat16)], axis=0
        )
        windows = extended[target.reshape(-1)].reshape(
            slot_count, trace_blocks, local_rcv, tap_count
        )
        returned = to_shots(windows)
        traces = returned[slot_index]
        terms = apply_filter(traces, adjoint_table, True)
        terms = terms.reshape(rows_here, shot_count, trace_blocks, local_rcv, tap_count).transpose(
            0, 3, 1, 2, 4
        )
        return terms.reshape(rows_here, local_rcv, shot_count, sample_count)

    tables = (
        time_table(sample_count),
        shot_table(slab_count * rows_here),
        shot_table(shot_count),
        shot_table(local_rcv * rcv_count),
    )
    row_bins = sample_count // 2 // slab_count
    rcv_bins = row_bins // rcv_count
    bin_start = lax.axis_index(("shot", "rep")) * row_bins + lax.axis_index("rcv") * rcv_bins

    def threshold_for(level_index):
        return lax.dynamic_slice_in_dim(thresholds[level_index], bin_start, rcv_bins)

    model_field = shrink(correlate(records), threshold_for(0), tables)
    level_index = 1
    traces = model_field.astype(jnp.bfloat16).reshape(
        rows_here, local_rcv, shot_count, trace_blocks, tap_count
    )
    traces = traces.transpose(0, 2, 3, 1, 4).reshape(
        rows_here * shot_count, trace_blocks, local_rcv, tap_count
    )
    shots = apply_filter(traces, forward_table, False).astype(jnp.bfloat16)
    outgoing = (
        jnp.zeros((slot_count, trace_blocks, local_rcv, tap_count), jnp.bfloat16)
        .at[slot_index]
        .set(shots)
    )
    arrived = to_slabs(outgoing)
    slab_total = jnp.zeros((slab_blocks + trace_blocks, local_rcv, tap_count), jnp.float32)
    for block_step in range(trace_blocks):
        slab_total = slab_total.at[target[:, block_step]].add(
            arrived[:, block_step].astype(jnp.float32)
        )
    spill_over = slab_total[slab_blocks : slab_blocks + trace_blocks - 1]
    carried = from_behind(spill_over, ("shot", "rep"), 1)
    blended = slab_total[:slab_blocks].at[: trace_blocks - 1].add(carried)
    residual = records - blended.transpose(1, 0, 2).reshape(local_rcv, slab_len)
    model_field = shrink(model_field + correlate(residual), threshold_for(level_index), tables)
    return (model_field, residual)


def dot(left, right, left_dim=1, right_dim=0):
    return lax.dot_general(
        left, right, (((left_dim,), (right_dim,)), ((), ())), preferred_element_type=jnp.float32
    )


def fixed_time_table(count):
    samples = np.arange(count)
    bins = np.arange(count // 2)[:, None]
    angles = 2.0 * np.pi / count * (bins * samples[None, :] % count)
    scale = math.sqrt(2.0 / count)
    cosine = scale * np.cos(angles)
    sine = -scale * np.sin(angles)
    cosine[0] = math.sqrt(1.0 / count)
    sine[0] = math.sqrt(1.0 / count) * np.where(samples % 2 == 0, 1.0, -1.0)
    return np.stack([cosine, sine]).astype(jnp.bfloat16)


def fixed_shot_table(count):
    positions = np.arange(count)
    angles = 2.0 * np.pi / count * (positions[:, None] * positions[None, :] % count)
    cosine = np.cos(angles) / math.sqrt(count)
    sine = np.sin(angles) / math.sqrt(count)
    table = np.stack([np.stack([cosine, sine], 1), np.stack([-sine, cosine], 1)])
    return table.astype(jnp.bfloat16).astype(np.float32)


def correlate_kernel(starts_ref, picks_ref, blocks_ref, tables_ref, out_ref):
    slots, rows, taps = out_ref.shape
    rcv = blocks_ref.shape[1]
    steps = rows // rcv

    def one(slot, carry):
        window = blocks_ref[pl.ds(starts_ref[slot], steps)].reshape(rows, taps)
        later = jnp.concatenate([window[rcv:], jnp.zeros((rcv, taps), window.dtype)], axis=0)
        pair = jnp.concatenate([window, later], axis=1)
        out_ref[slot] = dot(pair, tables_ref[picks_ref[slot]]).astype(out_ref.dtype)
        return carry

    lax.fori_loop(0, slots, one, 0, unroll=4)


def blend_kernel(starts_ref, picks_ref, traces_ref, tables_ref, out_ref):
    slots, rows, taps = traces_ref.shape
    rcv = out_ref.shape[1]
    steps = rows // rcv
    out_ref[...] = jnp.zeros_like(out_ref)

    def one(slot, carry):
        trace = traces_ref[slot]
        earlier = jnp.concatenate([jnp.zeros((rcv, taps), trace.dtype), trace[:-rcv]], axis=0)
        pair = jnp.concatenate([trace, earlier], axis=1)
        shot = dot(pair, tables_ref[picks_ref[slot]]).astype(jnp.bfloat16).astype(jnp.float32)
        where = pl.ds(starts_ref[slot], steps)
        out_ref[where] = out_ref[where] + shot.reshape(steps, rcv, taps)
        return carry

    lax.fori_loop(0, slots, one, 0, unroll=4)


def slot_call(kernel, out_shape, starts, picks, data, tables):
    vmem = pl.BlockSpec(memory_space=pltpu.VMEM)
    smem = pl.BlockSpec(memory_space=pltpu.SMEM)
    return pl.pallas_call(
        kernel,
        out_shape=out_shape,
        in_specs=[smem, smem, vmem, vmem],
        out_specs=vmem,
    )(starts, picks, data, tables)


def spectrum_kernel(traces_ref, table_ref, out_ref):
    parts, _, bins, _ = out_ref.shape
    both = dot(table_ref[...], traces_ref[0], 1, 1)
    half = parts * bins
    joined = jnp.concatenate([both[:half], both[half:]], axis=1)
    out_ref[:, 0] = joined.reshape(parts, bins, joined.shape[1]).astype(jnp.bfloat16)


def spectrum(traces, table, parts):
    rcv, slots, samples = traces.shape
    bins = samples // 2 // parts
    return pl.pallas_call(
        spectrum_kernel,
        grid=(rcv,),
        out_shape=jax.ShapeDtypeStruct((parts, rcv, bins, 2 * slots), jnp.bfloat16),
        in_specs=[
            pl.BlockSpec((1, slots, samples), lambda i: (i, 0, 0)),
            pl.BlockSpec((samples, samples), lambda i: (0, 0)),
        ],
        out_specs=pl.BlockSpec((parts, 1, bins, 2 * slots), lambda i: (0, i, 0, 0)),
    )(traces, table)


def record_kernel(spectra_ref, table_ref, out_ref):
    parts, _, bins, lanes = spectra_ref.shape
    half = parts * bins
    groups, _, count, _ = out_ref.shape
    values = spectra_ref[:, 0].reshape(half, lanes)
    first = dot(values, table_ref[:half], 0, 0)
    second = dot(values, table_ref[half:], 0, 0)
    for group in range(groups):
        low = 2 * group * count
        out_ref[group, 0] = first[low : low + count] + second[low + count : low + 2 * count]


def records_of(spectra, table, groups):
    parts, rcv, bins, lanes = spectra.shape
    samples = table.shape[1]
    count = lanes // 2 // groups
    return pl.pallas_call(
        record_kernel,
        grid=(rcv,),
        out_shape=jax.ShapeDtypeStruct((groups, rcv, count, samples), jnp.float32),
        in_specs=[
            pl.BlockSpec((parts, 1, bins, lanes), lambda i: (0, i, 0, 0)),
            pl.BlockSpec((samples, samples), lambda i: (0, 0)),
        ],
        out_specs=pl.BlockSpec((groups, 1, count, samples), lambda i: (0, i, 0, 0)),
    )(spectra, table)


def bins_kernel(place, halves, spectra_ref, go_ref, back_ref, cosine_ref, sine_ref, level_ref, out_ref):
    _, rcv, bins, lanes = spectra_ref.shape
    rows = rcv * bins
    rcv_count, slab_count = place.shape
    joined = jnp.concatenate(
        [
            jnp.concatenate(
                [spectra_ref[int(index)].reshape(rows, lanes) for index in line], axis=1
            )
            for line in place
        ],
        axis=0,
    )
    section = dot(joined, go_ref[...]).astype(jnp.bfloat16)
    half = section.shape[1] // 2
    near = dot(cosine_ref[...], section)
    far = dot(sine_ref[...], section)
    real = near[:, :half] + far[:, half:]
    imag = near[:, half:] - far[:, :half]
    level = level_ref[...]
    factor = 1.0 - level / jnp.maximum(jnp.sqrt(real * real + imag * imag), level)
    shrunk = jnp.concatenate([real * factor, imag * factor], axis=1).astype(jnp.bfloat16)
    near = dot(cosine_ref[...], shrunk)
    far = dot(sine_ref[...], shrunk)
    section = jnp.concatenate(
        [near[:, :half] - far[:, half:], far[:, :half] + near[:, half:]], axis=1
    ).astype(jnp.bfloat16)
    result = dot(section, back_ref[...], 1, 1).astype(jnp.bfloat16)
    width = result.shape[1] // slab_count
    for line in range(rcv_count):
        for slab in range(slab_count):
            piece = result[line * rows : (line + 1) * rows, slab * width : (slab + 1) * width]
            if halves == 2:
                piece = jnp.concatenate([piece[: rows // 2], piece[rows // 2 :]], axis=1)
            out_ref[int(place[line, slab])] = piece.reshape(rcv // halves, bins, halves * width)


def bins_stage(spectra, go, back, cosine, sine, level, place, halves):
    parts, rcv, bins, _ = spectra.shape
    width = halves * back.shape[0] // place.shape[1]
    vmem = pl.BlockSpec(memory_space=pltpu.VMEM)
    return pl.pallas_call(
        functools.partial(bins_kernel, place, halves),
        out_shape=jax.ShapeDtypeStruct((parts, rcv // halves, bins, width), jnp.bfloat16),
        in_specs=[vmem] * 6,
        out_specs=vmem,
    )(spectra, go, back, cosine, sine, level)


def body_by_slots(records, offsets, filter_index, signatures, thresholds):
    rows_here, shot_count = offsets.shape
    local_rcv, slab_len = records.shape
    slab_count = lax.axis_size(("shot", "rep"))
    rep_count = lax.axis_size("rep")
    rcv_count = lax.axis_size("rcv")
    parts = slab_count * rcv_count
    everyone = ("shot", "rcv", "rep")
    tap_count = signatures.shape[1]
    slab_blocks = slab_len // tap_count
    steps = NT // tap_count
    capacity = max(2, 2 * shot_count // slab_count)
    row_count = rows_here * slab_count
    slots = row_count * capacity
    bins = NT // 2 // parts
    place = np.array(
        [
            [((slab // rep_count) * rcv_count + line) * rep_count + slab % rep_count for slab in range(slab_count)]
            for line in range(rcv_count)
        ]
    )

    time_table_fixed = jnp.asarray(fixed_time_table(NT).reshape(NT, NT))
    table_x, table_y, table_r = (
        fixed_shot_table(count) for count in (row_count, shot_count, local_rcv * rcv_count)
    )
    grid_table = np.einsum("ajby,bkcx->cxyakj", table_y, table_x).astype(jnp.bfloat16)
    row_table = np.ascontiguousarray(grid_table.transpose(1, 0, 2, 3, 4, 5))
    points = 2 * row_count * shot_count
    grid_table = jnp.asarray(grid_table.reshape(points, points))
    row_table = jnp.asarray(row_table.reshape(points, points))
    same = np.eye(bins, dtype=np.float32)
    cosine = jnp.asarray(np.kron(table_r[0, :, 0], same).astype(jnp.bfloat16))
    sine = jnp.asarray(np.kron(table_r[0, :, 1], same).astype(jnp.bfloat16))

    shots = jnp.stack([offsets, filter_index])
    every = lax.all_to_all(
        jnp.broadcast_to(shots[None], (slab_count,) + shots.shape), ("shot", "rep"), 0, 0, tiled=True
    )
    every_offset = every[:, 0].reshape(row_count, shot_count)
    every_pick = every[:, 1].reshape(row_count, shot_count)
    every_owner = every_offset // slab_len
    every_rank = rank_in_row(every_owner)
    slabs = jnp.arange(slab_count, dtype=jnp.int32)
    ranks = jnp.arange(capacity, dtype=jnp.int32)
    taken = (every_owner[None, :, None, :] == slabs[:, None, None, None]) & (
        every_rank[None, :, None, :] == ranks[None, None, :, None]
    )
    point_of = jnp.arange(row_count * shot_count, dtype=jnp.int32).reshape(row_count, shot_count)
    code = jnp.sum(jnp.where(taken, point_of[None, :, None, :] + 1, 0), axis=3).reshape(
        slab_count, 1, slots
    )
    code = jnp.where(
        code > 0, code - 1 + row_count * shot_count * jnp.arange(2, dtype=jnp.int32)[None, :, None], -1
    ).reshape(-1)
    chosen = (code[:, None] == jnp.arange(points, dtype=jnp.int32)[None, :]).astype(jnp.bfloat16)
    slot_table = dot(chosen, grid_table).astype(jnp.bfloat16)
    mine = (every_owner == lax.axis_index(("shot", "rep")))[:, None, :] & (
        every_rank[:, None, :] == ranks[None, :, None]
    )
    every_start = every_offset // tap_count % slab_blocks
    starts = jnp.sum(jnp.where(mine, every_start[:, None, :], 0), axis=2).reshape(-1)
    picks = jnp.sum(jnp.where(mine, every_pick[:, None, :], 0), axis=2).reshape(-1)
    forward_tables, adjoint_tables = toeplitz_tables(signatures)

    def correlate(blocks, dtype):
        low = blocks.astype(jnp.bfloat16)
        rim = from_behind(low[: steps - 1], ("shot", "rep"), -1)
        extended = jnp.concatenate([low, rim, jnp.zeros_like(low[:1])], axis=0)
        shape = jax.ShapeDtypeStruct((slots, steps * local_rcv, tap_count), dtype)
        terms = slot_call(correlate_kernel, shape, starts, picks, extended, adjoint_tables)
        terms = terms.reshape(slots, steps, local_rcv, tap_count).transpose(2, 0, 1, 3)
        return terms.reshape(local_rcv, slots, NT)

    bin_start = lax.axis_index(everyone) * bins

    def swap(value):
        return lax.all_to_all(value, everyone, 0, 0, tiled=True)

    def shrink_at(traces, index, back, halves):
        level = lax.dynamic_slice_in_dim(thresholds[index], bin_start, bins)
        level = jnp.tile(level, local_rcv * rcv_count)[:, None]
        spectra = swap(spectrum(traces, time_table_fixed, parts))
        spectra = swap(
            bins_stage(spectra, slot_table, back, cosine, sine, level, place, halves)
        )
        return records_of(spectra, time_table_fixed, halves)

    record_blocks = records.reshape(local_rcv, slab_blocks, tap_count).transpose(1, 0, 2)
    model = shrink_at(correlate(record_blocks, jnp.bfloat16), 0, slot_table, 1)[0]
    traces = model.astype(jnp.bfloat16).reshape(local_rcv, slots, steps, tap_count)
    traces = traces.transpose(1, 2, 0, 3).reshape(slots, steps * local_rcv, tap_count)
    shape = jax.ShapeDtypeStruct((slab_blocks + steps, local_rcv, tap_count), jnp.float32)
    total = slot_call(blend_kernel, shape, starts, picks, traces, forward_tables)
    carried = from_behind(total[slab_blocks : slab_blocks + steps - 1], ("shot", "rep"), 1)
    blended = total[:slab_blocks].at[: steps - 1].add(carried)
    left = record_blocks - blended
    residual = left.transpose(1, 0, 2).reshape(local_rcv, slab_len)
    traces = (model + correlate(left, jnp.float32)).astype(jnp.bfloat16)
    model = shrink_at(traces, 1, row_table, 2)
    return (model.reshape(rows_here, local_rcv, shot_count, NT), residual)


def body(records, offsets, filter_index, signatures, thresholds):
    rows_here, shot_count = offsets.shape
    slab_count = lax.axis_size(("shot", "rep"))
    parts = slab_count * lax.axis_size("rcv")
    slots = rows_here * slab_count * max(2, 2 * shot_count // slab_count)
    table_rows = 2 * rows_here * slab_count * shot_count
    fits = table_rows <= 1024 and rows_here == 1 and slots == 64 and 4 * shot_count == 128
    fits = fits and records.shape[0] == 16 and NT // 2 // parts == 16
    run = body_by_slots if fits else body_by_rows
    return run(records, offsets, filter_index, signatures, thresholds)


def solution(mesh):
    in_specs = (
        P(("groups", "rcv"), ("shot", "rep")),
        P(("groups", "shot", "rep"), None),
        P(("groups", "shot", "rep"), None),
        P(),
        P(),
    )
    out_specs = (
        P(("groups", "shot", "rep"), "rcv", None, None),
        P(("groups", "rcv"), ("shot", "rep")),
    )
    return jax.shard_map(body, mesh=mesh, in_specs=in_specs, out_specs=out_specs, check_vma=False)
```

```python
import functools
import math

import jax
import jax.numpy as jnp
import numpy as np
from jax import lax
from jax.experimental import pallas as pl
from jax.experimental.pallas import tpu as pltpu
from jax.sharding import PartitionSpec as P

NT = 512


def from_behind(value, axis, steps):
    count = lax.axis_size(axis)
    first, last = (max(0, -steps), min(count, count - steps))
    return lax.ppermute(value, axis, [(source, source + steps) for source in range(first, last)])


def time_table(count):
    samples = jnp.arange(count)
    bin_index = jnp.arange(count // 2)[:, None]
    angles = 2.0 * math.pi / count * (bin_index * samples[None, :] % count).astype(jnp.float32)
    parity = jnp.where(samples % 2 == 0, 1.0, -1.0).astype(jnp.float32)
    cosine = jnp.where(bin_index == 0, math.sqrt(1.0 / count), math.sqrt(2.0 / count)) * jnp.cos(
        angles
    )
    sine_part = jnp.where(
        bin_index == 0,
        math.sqrt(1.0 / count) * parity[None, :],
        -math.sqrt(2.0 / count) * jnp.sin(angles),
    )
    return jnp.stack([cosine, sine_part]).astype(jnp.bfloat16)


def shot_table(count):
    positions = jnp.arange(count)
    angles = (
        2.0
        * math.pi
        / count
        * (positions[:, None] * positions[None, :] % count).astype(jnp.float32)
    )
    scaling = 1.0 / math.sqrt(count)
    cosine = scaling * jnp.cos(angles)
    sine_part = scaling * jnp.sin(angles)
    upper_half = jnp.stack([cosine, sine_part], axis=1)
    lower_half = jnp.stack([-sine_part, cosine], axis=1)
    return jnp.stack([upper_half, lower_half]).astype(jnp.bfloat16)


def toeplitz_kernel(taps_ref, forward_ref, adjoint_ref):
    tap_count = taps_ref.shape[1]
    row_index = lax.broadcasted_iota(jnp.int32, (tap_count, tap_count), 0)
    col_index = lax.broadcasted_iota(jnp.int32, (tap_count, tap_count), 1)
    for index in range(taps_ref.shape[0]):
        row = jnp.broadcast_to(taps_ref[index : index + 1, :], (tap_count, tap_count))
        turned = pltpu.roll(row, 0, 1, stride=1, stride_axis=0)
        zeros = jnp.zeros_like(turned)
        near = jnp.where(col_index >= row_index, turned, zeros)
        far = jnp.where(col_index < row_index, turned, zeros)
        forward_ref[index, :tap_count, :] = near.astype(jnp.bfloat16)
        forward_ref[index, tap_count:, :] = far.astype(jnp.bfloat16)
        adjoint_ref[index, :tap_count, :] = near.T.astype(jnp.bfloat16)
        adjoint_ref[index, tap_count:, :] = far.T.astype(jnp.bfloat16)


def toeplitz_tables(signatures):
    count, tap_count = signatures.shape
    shape = jax.ShapeDtypeStruct((count, 2 * tap_count, tap_count), jnp.bfloat16)
    return pl.pallas_call(
        toeplitz_kernel,
        out_shape=(shape, shape),
        in_specs=[pl.BlockSpec(memory_space=pltpu.VMEM)],
        out_specs=(pl.BlockSpec(memory_space=pltpu.VMEM),) * 2,
    )(signatures.astype(jnp.float32))


def apply_filter(traces, table, adjoint):
    empty = jnp.zeros_like(traces[:, :1])
    if adjoint:
        other = jnp.concatenate([traces[:, 1:], empty], axis=1)
    else:
        other = jnp.concatenate([empty, traces[:, :-1]], axis=1)
    return jnp.einsum(
        "sbrp,spq->sbrq",
        jnp.concatenate([traces, other], axis=3),
        table,
        preferred_element_type=jnp.float32,
    )


def rank_in_row(owners):
    shot_count = owners.shape[1]
    same_owner = owners[:, :, None] == owners[:, None, :]
    earlier = jnp.arange(shot_count)[None, :] < jnp.arange(shot_count)[:, None]
    return jnp.sum(same_owner & earlier[None], axis=2)


def to_slabs(payload):
    return lax.all_to_all(payload, ("shot", "rep"), split_axis=0, concat_axis=0, tiled=True)


def to_shots(payload):
    return lax.all_to_all(payload, ("shot", "rep"), split_axis=0, concat_axis=0, tiled=True)


def soft_limit(coefficients, threshold_row):
    magnitude = jnp.sqrt(coefficients[0] * coefficients[0] + coefficients[1] * coefficients[1])
    threshold_view = threshold_row[None, :, None, None]
    factor = 1.0 - threshold_view / jnp.maximum(magnitude, threshold_view)
    return (coefficients * factor[None]).astype(jnp.bfloat16)


def shrink(field_data, threshold_row, tables):
    table_time, table_x, table_y, table_r = tables
    rows_here, local_rcv, shot_count, sample_count = field_data.shape
    spectrum = jnp.einsum(
        "ckt,xryt->xckry",
        table_time,
        field_data.astype(jnp.bfloat16),
        preferred_element_type=jnp.float32,
    ).astype(jnp.bfloat16)
    bin_count = spectrum.shape[2]
    spectrum = spectrum.reshape(rows_here, 2, bin_count, local_rcv * shot_count)
    section_data = jnp.einsum(
        "akbx,xbfz->akfz",
        table_x,
        lax.all_to_all(spectrum, ("shot", "rep"), split_axis=2, concat_axis=0, tiled=True),
        preferred_element_type=jnp.float32,
    ).astype(jnp.bfloat16)
    all_rows, row_bins = (section_data.shape[1], section_data.shape[2])
    section_data = section_data.reshape(2, all_rows, row_bins, local_rcv, shot_count)
    section_data = lax.all_to_all(section_data, "rcv", split_axis=2, concat_axis=3, tiled=True)
    section_data = jnp.einsum(
        "ajby,bkfry->akfrj", table_y, section_data, preferred_element_type=jnp.float32
    ).astype(jnp.bfloat16)
    coefficients = jnp.einsum(
        "aqbr,bkfrj->akfqj", table_r, section_data, preferred_element_type=jnp.float32
    )
    shrunk = soft_limit(coefficients, threshold_row)
    section_data = jnp.einsum(
        "aqbr,akfqj->bkfrj", table_r, shrunk, preferred_element_type=jnp.float32
    ).astype(jnp.bfloat16)
    section_data = jnp.einsum(
        "ajby,akfrj->bkfry", table_y, section_data, preferred_element_type=jnp.float32
    ).astype(jnp.bfloat16)
    section_data = lax.all_to_all(section_data, "rcv", split_axis=3, concat_axis=2, tiled=True)
    section_data = section_data.reshape(2, all_rows, row_bins, local_rcv * shot_count)
    section_data = jnp.einsum(
        "akbx,akfz->bxfz", table_x, section_data, preferred_element_type=jnp.float32
    ).astype(jnp.bfloat16)
    result = jnp.einsum(
        "ckt,cxkz->xzt",
        table_time,
        lax.all_to_all(section_data, ("shot", "rep"), split_axis=1, concat_axis=2, tiled=True),
        preferred_element_type=jnp.float32,
    )
    return result.reshape(rows_here, local_rcv, shot_count, sample_count)


def body_by_rows(records, offsets, filter_index, signatures, thresholds):
    rows_here, shot_count = offsets.shape
    local_rcv, slab_len = records.shape
    slab_count = lax.axis_size(("shot", "rep"))
    rcv_count = lax.axis_size("rcv")
    tap_count = signatures.shape[1]
    sample_count = NT
    slab_blocks = slab_len // tap_count
    trace_blocks = sample_count // tap_count
    capacity = max(2, 2 * shot_count // slab_count)
    slot_count = slab_count * rows_here * capacity
    forward_tables, adjoint_tables = toeplitz_tables(signatures)
    flat_index = filter_index.reshape(-1)
    forward_table = forward_tables[flat_index]
    adjoint_table = adjoint_tables[flat_index]
    owners = offsets // slab_len
    row_ids = jnp.arange(rows_here, dtype=jnp.int32)[:, None]
    slot_index = (
        owners * (rows_here * capacity) + row_ids * capacity + rank_in_row(owners)
    ).reshape(-1)
    every_offset = lax.all_gather(offsets, ("shot", "rep"), axis=0, tiled=True)
    every_owner = every_offset // slab_len
    every_start = every_offset // tap_count % slab_blocks
    every_rank = rank_in_row(every_owner)
    mine_mask = every_owner == lax.axis_index(("shot", "rep"))
    levels = jnp.arange(capacity, dtype=jnp.int32)
    picked = mine_mask[:, :, None] & (every_rank[:, :, None] == levels[None, None, :])
    table_in = jnp.sum(jnp.where(picked, every_start[:, :, None] + 1, 0), axis=1).reshape(-1)
    filled = table_in > 0
    block_steps = jnp.arange(trace_blocks, dtype=jnp.int32)
    target = jnp.where(
        filled[:, None],
        table_in[:, None] - 1 + block_steps[None, :],
        slab_blocks + trace_blocks - 1,
    )

    def correlate(record_field):
        record_low = (
            record_field.astype(jnp.bfloat16)
            .reshape(local_rcv, slab_blocks, tap_count)
            .transpose(1, 0, 2)
        )
        rim_blocks = from_behind(record_low[: trace_blocks - 1], ("shot", "rep"), -1)
        extended = jnp.concatenate(
            [record_low, rim_blocks, jnp.zeros((1, local_rcv, tap_count), jnp.bfloat16)], axis=0
        )
        windows = extended[target.reshape(-1)].reshape(
            slot_count, trace_blocks, local_rcv, tap_count
        )
        returned = to_shots(windows)
        traces = returned[slot_index]
        terms = apply_filter(traces, adjoint_table, True)
        terms = terms.reshape(rows_here, shot_count, trace_blocks, local_rcv, tap_count).transpose(
            0, 3, 1, 2, 4
        )
        return terms.reshape(rows_here, local_rcv, shot_count, sample_count)

    tables = (
        time_table(sample_count),
        shot_table(slab_count * rows_here),
        shot_table(shot_count),
        shot_table(local_rcv * rcv_count),
    )
    row_bins = sample_count // 2 // slab_count
    rcv_bins = row_bins // rcv_count
    bin_start = lax.axis_index(("shot", "rep")) * row_bins + lax.axis_index("rcv") * rcv_bins

    def threshold_for(level_index):
        return lax.dynamic_slice_in_dim(thresholds[level_index], bin_start, rcv_bins)

    model_field = shrink(correlate(records), threshold_for(0), tables)
    level_index = 1
    traces = model_field.astype(jnp.bfloat16).reshape(
        rows_here, local_rcv, shot_count, trace_blocks, tap_count
    )
    traces = traces.transpose(0, 2, 3, 1, 4).reshape(
        rows_here * shot_count, trace_blocks, local_rcv, tap_count
    )
    shots = apply_filter(traces, forward_table, False).astype(jnp.bfloat16)
    outgoing = (
        jnp.zeros((slot_count, trace_blocks, local_rcv, tap_count), jnp.bfloat16)
        .at[slot_index]
        .set(shots)
    )
    arrived = to_slabs(outgoing)
    slab_total = jnp.zeros((slab_blocks + trace_blocks, local_rcv, tap_count), jnp.float32)
    for block_step in range(trace_blocks):
        slab_total = slab_total.at[target[:, block_step]].add(
            arrived[:, block_step].astype(jnp.float32)
        )
    spill_over = slab_total[slab_blocks : slab_blocks + trace_blocks - 1]
    carried = from_behind(spill_over, ("shot", "rep"), 1)
    blended = slab_total[:slab_blocks].at[: trace_blocks - 1].add(carried)
    residual = records - blended.transpose(1, 0, 2).reshape(local_rcv, slab_len)
    model_field = shrink(model_field + correlate(residual), threshold_for(level_index), tables)
    return (model_field, residual)


def dot(left, right, left_dim=1, right_dim=0):
    return lax.dot_general(
        left, right, (((left_dim,), (right_dim,)), ((), ())), preferred_element_type=jnp.float32
    )


def fixed_time_table(count):
    samples = np.arange(count)
    bins = np.arange(count // 2)[:, None]
    angles = 2.0 * np.pi / count * (bins * samples[None, :] % count)
    scale = math.sqrt(2.0 / count)
    cosine = scale * np.cos(angles)
    sine = -scale * np.sin(angles)
    cosine[0] = math.sqrt(1.0 / count)
    sine[0] = math.sqrt(1.0 / count) * np.where(samples % 2 == 0, 1.0, -1.0)
    return np.stack([cosine, sine]).astype(jnp.bfloat16)


def fixed_shot_table(count):
    positions = np.arange(count)
    angles = 2.0 * np.pi / count * (positions[:, None] * positions[None, :] % count)
    cosine = np.cos(angles) / math.sqrt(count)
    sine = np.sin(angles) / math.sqrt(count)
    table = np.stack([np.stack([cosine, sine], 1), np.stack([-sine, cosine], 1)])
    return table.astype(jnp.bfloat16).astype(np.float32)


def analyse(with_model, starts_ref, picks_ref, blocks_ref, taps_ref, table_ref, *rest):
    model_ref = rest[0] if with_model else None
    out_ref, held_ref = rest[-2:]
    rcv, taps = blocks_ref.shape[1:]
    parts, _, bins, lanes = out_ref.shape
    slots = lanes // 2
    rows = held_ref.shape[0] // slots
    steps = rows // rcv
    half = parts * bins

    def one(slot, carry):
        window = blocks_ref[pl.ds(starts_ref[slot], steps)].reshape(rows, taps)
        later = jnp.concatenate([window[rcv:], jnp.zeros((rcv, taps), window.dtype)], axis=0)
        pair = jnp.concatenate([window, later], axis=1)
        terms = dot(pair, taps_ref[picks_ref[slot]])
        where = pl.ds(pl.multiple_of(slot * rows, rows), rows)
        if with_model:
            terms = terms + model_ref[where]
        held_ref[where] = terms
        return carry

    lax.fori_loop(0, slots, one, 0, unroll=8)
    together = math.gcd(rcv, 4)
    for first in range(0, rcv, together):
        traces = jnp.concatenate(
            [
                jnp.concatenate(
                    [
                        held_ref[pl.ds(step * rcv + line, slots, stride=rows), :].astype(jnp.bfloat16)
                        for step in range(steps)
                    ],
                    axis=1,
                )
                for line in range(first, first + together)
            ],
            axis=0,
        )
        both = dot(table_ref[...], traces, 1, 1)
        for line in range(together):
            piece = both[:, line * slots : (line + 1) * slots]
            joined = jnp.concatenate([piece[:half], piece[half:]], axis=1)
            out_ref[:, first + line] = joined.reshape(parts, bins, lanes).astype(jnp.bfloat16)


def slots_to_spectra(starts, picks, blocks, taps, table, model, parts, slots):
    rcv, width = blocks.shape[1:]
    samples = table.shape[1]
    vmem = pl.BlockSpec(memory_space=pltpu.VMEM)
    smem = pl.BlockSpec(memory_space=pltpu.SMEM)
    extra = () if model is None else (model,)
    return pl.pallas_call(
        functools.partial(analyse, model is not None),
        out_shape=jax.ShapeDtypeStruct((parts, rcv, samples // 2 // parts, 2 * slots), jnp.bfloat16),
        in_specs=[smem, smem, vmem, vmem, vmem] + [vmem] * len(extra),
        out_specs=vmem,
        scratch_shapes=[pltpu.VMEM((slots * rcv * samples // width, width), jnp.float32)],
    )(starts, picks, blocks, taps, table, *extra)


def upright(spectra_ref, lines, group_lanes):
    parts, _, bins, _ = spectra_ref.shape
    pieces = []
    for line in lines:
        turned = spectra_ref[:, line].reshape(parts * bins, -1).astype(jnp.float32).T
        turned = turned.astype(jnp.bfloat16)
        count = group_lanes // 2
        for low in range(0, turned.shape[0], group_lanes):
            pieces.append(
                jnp.concatenate(
                    [turned[low : low + count], turned[low + count : low + 2 * count]], axis=1
                )
            )
    return jnp.concatenate(pieces, axis=0)


def synthesise(starts_ref, picks_ref, spectra_ref, taps_ref, table_ref, model_ref, total_ref):
    rcv, lanes = spectra_ref.shape[1], spectra_ref.shape[3]
    slots = lanes // 2
    taps = model_ref.shape[1]
    rows = model_ref.shape[0] // slots
    steps = rows // rcv
    together = math.gcd(rcv, 4)
    for first in range(0, rcv, together):
        lines = range(first, first + together)
        fields = dot(upright(spectra_ref, lines, lanes), table_ref[...])
        for line in lines:
            low = (line - first) * slots
            for step in range(steps):
                model_ref[pl.ds(step * rcv + line, slots, stride=rows), :] = fields[
                    low : low + slots, step * taps : (step + 1) * taps
                ]
    total_ref[...] = jnp.zeros_like(total_ref)

    def one(slot, carry):
        trace = model_ref[pl.ds(pl.multiple_of(slot * rows, rows), rows)].astype(jnp.bfloat16)
        earlier = jnp.concatenate([jnp.zeros((rcv, taps), trace.dtype), trace[:-rcv]], axis=0)
        pair = jnp.concatenate([trace, earlier], axis=1)
        shot = dot(pair, taps_ref[picks_ref[slot]]).astype(jnp.bfloat16).astype(jnp.float32)
        where = pl.ds(starts_ref[slot], steps)
        total_ref[where] = total_ref[where] + shot.reshape(steps, rcv, taps)
        return carry

    lax.fori_loop(0, slots, one, 0, unroll=8)


def spectra_to_slab(starts, picks, spectra, taps, table, slab_blocks):
    _, rcv, _, lanes = spectra.shape
    width = taps.shape[2]
    steps = table.shape[1] // width
    vmem = pl.BlockSpec(memory_space=pltpu.VMEM)
    smem = pl.BlockSpec(memory_space=pltpu.SMEM)
    return pl.pallas_call(
        synthesise,
        out_shape=(
            jax.ShapeDtypeStruct((lanes // 2 * rcv * steps, width), jnp.float32),
            jax.ShapeDtypeStruct((slab_blocks + steps, rcv, width), jnp.float32),
        ),
        in_specs=[smem, smem, vmem, vmem, vmem],
        out_specs=(vmem, vmem),
    )(starts, picks, spectra, taps, table)


def record_kernel(groups, spectra_ref, table_ref, out_ref):
    count = out_ref.shape[2]
    together = spectra_ref.shape[1]
    fields = dot(upright(spectra_ref, range(together), 2 * count), table_ref[...])
    for line in range(together):
        for group in range(groups):
            low = (line * groups + group) * count
            out_ref[group, line] = fields[low : low + count]


def records_of(spectra, table, groups):
    parts, rcv, bins, lanes = spectra.shape
    samples = table.shape[1]
    count = lanes // 2 // groups
    together = math.gcd(rcv, 4)
    return pl.pallas_call(
        functools.partial(record_kernel, groups),
        grid=(rcv // together,),
        out_shape=jax.ShapeDtypeStruct((groups, rcv, count, samples), jnp.float32),
        in_specs=[
            pl.BlockSpec((parts, together, bins, lanes), lambda i: (0, i, 0, 0)),
            pl.BlockSpec((samples, samples), lambda i: (0, 0)),
        ],
        out_specs=pl.BlockSpec((groups, together, count, samples), lambda i: (0, i, 0, 0)),
    )(spectra, table)


def bins_kernel(place, halves, spectra_ref, go_ref, back_ref, cosine_ref, sine_ref, level_ref, out_ref):
    _, rcv, bins, lanes = spectra_ref.shape
    rows = rcv * bins
    rcv_count, slab_count = place.shape
    joined = jnp.concatenate(
        [
            jnp.concatenate(
                [spectra_ref[int(index)].reshape(rows, lanes) for index in line], axis=1
            )
            for line in place
        ],
        axis=0,
    )
    section = dot(joined, go_ref[...]).astype(jnp.bfloat16)
    half = section.shape[1] // 2
    near = dot(cosine_ref[...], section)
    far = dot(sine_ref[...], section)
    real = near[:, :half] + far[:, half:]
    imag = near[:, half:] - far[:, :half]
    level = level_ref[...]
    factor = 1.0 - level / jnp.maximum(jnp.sqrt(real * real + imag * imag), level)
    shrunk = jnp.concatenate([real * factor, imag * factor], axis=1).astype(jnp.bfloat16)
    near = dot(cosine_ref[...], shrunk)
    far = dot(sine_ref[...], shrunk)
    section = jnp.concatenate(
        [near[:, :half] - far[:, half:], far[:, :half] + near[:, half:]], axis=1
    ).astype(jnp.bfloat16)
    result = dot(section, back_ref[...], 1, 1).astype(jnp.bfloat16)
    width = result.shape[1] // slab_count
    for line in range(rcv_count):
        for slab in range(slab_count):
            piece = result[line * rows : (line + 1) * rows, slab * width : (slab + 1) * width]
            if halves == 2:
                piece = jnp.concatenate([piece[: rows // 2], piece[rows // 2 :]], axis=1)
            out_ref[int(place[line, slab])] = piece.reshape(rcv // halves, bins, halves * width)


def bins_stage(spectra, go, back, cosine, sine, level, place, halves):
    parts, rcv, bins, _ = spectra.shape
    width = halves * back.shape[0] // place.shape[1]
    vmem = pl.BlockSpec(memory_space=pltpu.VMEM)
    return pl.pallas_call(
        functools.partial(bins_kernel, place, halves),
        out_shape=jax.ShapeDtypeStruct((parts, rcv // halves, bins, width), jnp.bfloat16),
        in_specs=[vmem] * 6,
        out_specs=vmem,
    )(spectra, go, back, cosine, sine, level)


def body_by_slots(records, offsets, filter_index, signatures, thresholds):
    rows_here, shot_count = offsets.shape
    local_rcv, slab_len = records.shape
    slab_count = lax.axis_size(("shot", "rep"))
    rep_count = lax.axis_size("rep")
    rcv_count = lax.axis_size("rcv")
    parts = slab_count * rcv_count
    everyone = ("shot", "rcv", "rep")
    tap_count = signatures.shape[1]
    slab_blocks = slab_len // tap_count
    steps = NT // tap_count
    capacity = max(2, 2 * shot_count // slab_count)
    row_count = rows_here * slab_count
    slots = row_count * capacity
    bins = NT // 2 // parts
    place = np.array(
        [
            [((slab // rep_count) * rcv_count + line) * rep_count + slab % rep_count for slab in range(slab_count)]
            for line in range(rcv_count)
        ]
    )

    time_table_fixed = jnp.asarray(fixed_time_table(NT).reshape(NT, NT))
    table_x, table_y, table_r = (
        fixed_shot_table(count) for count in (row_count, shot_count, local_rcv * rcv_count)
    )
    grid_table = np.einsum("ajby,bkcx->cxyakj", table_y, table_x).astype(jnp.bfloat16)
    row_table = np.ascontiguousarray(grid_table.transpose(1, 0, 2, 3, 4, 5))
    points = 2 * row_count * shot_count
    grid_table = jnp.asarray(grid_table.reshape(points, points))
    row_table = jnp.asarray(row_table.reshape(points, points))
    same = np.eye(bins, dtype=np.float32)
    cosine = jnp.asarray(np.kron(table_r[0, :, 0], same).astype(jnp.bfloat16))
    sine = jnp.asarray(np.kron(table_r[0, :, 1], same).astype(jnp.bfloat16))

    shots = jnp.stack([offsets, filter_index])
    every = lax.all_to_all(
        jnp.broadcast_to(shots[None], (slab_count,) + shots.shape), ("shot", "rep"), 0, 0, tiled=True
    )
    every_offset = every[:, 0].reshape(row_count, shot_count)
    every_pick = every[:, 1].reshape(row_count, shot_count)
    every_owner = every_offset // slab_len
    every_rank = rank_in_row(every_owner)
    slabs = jnp.arange(slab_count, dtype=jnp.int32)
    ranks = jnp.arange(capacity, dtype=jnp.int32)
    taken = (every_owner[None, :, None, :] == slabs[:, None, None, None]) & (
        every_rank[None, :, None, :] == ranks[None, None, :, None]
    )
    point_of = jnp.arange(row_count * shot_count, dtype=jnp.int32).reshape(row_count, shot_count)
    code = jnp.sum(jnp.where(taken, point_of[None, :, None, :] + 1, 0), axis=3).reshape(
        slab_count, 1, slots
    )
    code = jnp.where(
        code > 0, code - 1 + row_count * shot_count * jnp.arange(2, dtype=jnp.int32)[None, :, None], -1
    ).reshape(-1)
    chosen = (code[:, None] == jnp.arange(points, dtype=jnp.int32)[None, :]).astype(jnp.bfloat16)
    slot_table = dot(chosen, grid_table).astype(jnp.bfloat16)
    mine = (every_owner == lax.axis_index(("shot", "rep")))[:, None, :] & (
        every_rank[:, None, :] == ranks[None, :, None]
    )
    every_start = every_offset // tap_count % slab_blocks
    starts = jnp.sum(jnp.where(mine, every_start[:, None, :], 0), axis=2).reshape(-1)
    picks = jnp.sum(jnp.where(mine, every_pick[:, None, :], 0), axis=2).reshape(-1)
    forward_tables, adjoint_tables = toeplitz_tables(signatures)

    def correlate(blocks, model):
        low = blocks.astype(jnp.bfloat16)
        rim = from_behind(low[: steps - 1], ("shot", "rep"), -1)
        extended = jnp.concatenate([low, rim, jnp.zeros_like(low[:1])], axis=0)
        return slots_to_spectra(
            starts, picks, extended, adjoint_tables, time_table_fixed, model, parts, slots
        )

    bin_start = lax.axis_index(everyone) * bins

    def swap(value):
        return lax.all_to_all(value, everyone, 0, 0, tiled=True)

    def shrink_at(spectra, index, back, halves):
        level = lax.dynamic_slice_in_dim(thresholds[index], bin_start, bins)
        level = jnp.tile(level, local_rcv * rcv_count)[:, None]
        return swap(
            bins_stage(swap(spectra), slot_table, back, cosine, sine, level, place, halves)
        )

    record_blocks = records.reshape(local_rcv, slab_blocks, tap_count).transpose(1, 0, 2)
    spectra = shrink_at(correlate(record_blocks, None), 0, slot_table, 1)
    model, total = spectra_to_slab(
        starts, picks, spectra, forward_tables, time_table_fixed, slab_blocks
    )
    carried = from_behind(total[slab_blocks : slab_blocks + steps - 1], ("shot", "rep"), 1)
    blended = total[:slab_blocks].at[: steps - 1].add(carried)
    left = record_blocks - blended
    residual = left.transpose(1, 0, 2).reshape(local_rcv, slab_len)
    spectra = shrink_at(correlate(left, model), 1, row_table, 2)
    model = records_of(spectra, time_table_fixed, 2)
    return (model.reshape(rows_here, local_rcv, shot_count, NT), residual)


def body(records, offsets, filter_index, signatures, thresholds):
    rows_here, shot_count = offsets.shape
    slab_count = lax.axis_size(("shot", "rep"))
    parts = slab_count * lax.axis_size("rcv")
    slots = rows_here * slab_count * max(2, 2 * shot_count // slab_count)
    table_rows = 2 * rows_here * slab_count * shot_count
    fits = table_rows <= 1024 and rows_here == 1 and slots == 64 and 4 * shot_count == 128
    fits = fits and records.shape[0] == 16 and NT // 2 // parts == 16
    run = body_by_slots if fits else body_by_rows
    return run(records, offsets, filter_index, signatures, thresholds)


def solution(mesh):
    in_specs = (
        P(("groups", "rcv"), ("shot", "rep")),
        P(("groups", "shot", "rep"), None),
        P(("groups", "shot", "rep"), None),
        P(),
        P(),
    )
    out_specs = (
        P(("groups", "shot", "rep"), "rcv", None, None),
        P(("groups", "rcv"), ("shot", "rep")),
    )
    return jax.shard_map(body, mesh=mesh, in_specs=in_specs, out_specs=out_specs, check_vma=False)
```

```python
import functools
import math

import jax
import jax.numpy as jnp
import numpy as np
from jax import lax
from jax.experimental import pallas as pl
from jax.experimental.pallas import tpu as pltpu
from jax.sharding import PartitionSpec as P

NT = 512


def from_behind(value, axis, steps):
    count = lax.axis_size(axis)
    first, last = (max(0, -steps), min(count, count - steps))
    return lax.ppermute(value, axis, [(source, source + steps) for source in range(first, last)])


def time_table(count):
    samples = jnp.arange(count)
    bin_index = jnp.arange(count // 2)[:, None]
    angles = 2.0 * math.pi / count * (bin_index * samples[None, :] % count).astype(jnp.float32)
    parity = jnp.where(samples % 2 == 0, 1.0, -1.0).astype(jnp.float32)
    cosine = jnp.where(bin_index == 0, math.sqrt(1.0 / count), math.sqrt(2.0 / count)) * jnp.cos(
        angles
    )
    sine_part = jnp.where(
        bin_index == 0,
        math.sqrt(1.0 / count) * parity[None, :],
        -math.sqrt(2.0 / count) * jnp.sin(angles),
    )
    return jnp.stack([cosine, sine_part]).astype(jnp.bfloat16)


def shot_table(count):
    positions = jnp.arange(count)
    angles = (
        2.0
        * math.pi
        / count
        * (positions[:, None] * positions[None, :] % count).astype(jnp.float32)
    )
    scaling = 1.0 / math.sqrt(count)
    cosine = scaling * jnp.cos(angles)
    sine_part = scaling * jnp.sin(angles)
    upper_half = jnp.stack([cosine, sine_part], axis=1)
    lower_half = jnp.stack([-sine_part, cosine], axis=1)
    return jnp.stack([upper_half, lower_half]).astype(jnp.bfloat16)


def toeplitz_kernel(adjoint, taps_ref, out_ref):
    tap_count = taps_ref.shape[1]
    row_index = lax.broadcasted_iota(jnp.int32, (tap_count, tap_count), 0)
    col_index = lax.broadcasted_iota(jnp.int32, (tap_count, tap_count), 1)
    taps = taps_ref[...].astype(jnp.float32)
    for index in range(taps_ref.shape[0]):
        row = jnp.broadcast_to(taps[index : index + 1, :], (tap_count, tap_count))
        turned = pltpu.roll(row, 0, 1, stride=1, stride_axis=0)
        zeros = jnp.zeros_like(turned)
        near = jnp.where(col_index >= row_index, turned, zeros)
        far = jnp.where(col_index < row_index, turned, zeros)
        near, far = (near.T, far.T) if adjoint else (near, far)
        out_ref[index, :tap_count, :] = near.astype(jnp.bfloat16)
        out_ref[index, tap_count:, :] = far.astype(jnp.bfloat16)


def toeplitz_table(signatures, adjoint):
    count, tap_count = signatures.shape
    return pl.pallas_call(
        functools.partial(toeplitz_kernel, adjoint),
        out_shape=jax.ShapeDtypeStruct((count, 2 * tap_count, tap_count), jnp.bfloat16),
        in_specs=[pl.BlockSpec(memory_space=pltpu.VMEM)],
        out_specs=pl.BlockSpec(memory_space=pltpu.VMEM),
    )(signatures)


def apply_filter(traces, table, adjoint):
    empty = jnp.zeros_like(traces[:, :1])
    if adjoint:
        other = jnp.concatenate([traces[:, 1:], empty], axis=1)
    else:
        other = jnp.concatenate([empty, traces[:, :-1]], axis=1)
    return jnp.einsum(
        "sbrp,spq->sbrq",
        jnp.concatenate([traces, other], axis=3),
        table,
        preferred_element_type=jnp.float32,
    )


def rank_in_row(owners):
    shot_count = owners.shape[1]
    same_owner = owners[:, :, None] == owners[:, None, :]
    earlier = jnp.arange(shot_count)[None, :] < jnp.arange(shot_count)[:, None]
    return jnp.sum(same_owner & earlier[None], axis=2)


def to_slabs(payload):
    return lax.all_to_all(payload, ("shot", "rep"), split_axis=0, concat_axis=0, tiled=True)


def to_shots(payload):
    return lax.all_to_all(payload, ("shot", "rep"), split_axis=0, concat_axis=0, tiled=True)


def soft_limit(coefficients, threshold_row):
    magnitude = jnp.sqrt(coefficients[0] * coefficients[0] + coefficients[1] * coefficients[1])
    threshold_view = threshold_row[None, :, None, None]
    factor = 1.0 - threshold_view / jnp.maximum(magnitude, threshold_view)
    return (coefficients * factor[None]).astype(jnp.bfloat16)


def shrink(field_data, threshold_row, tables):
    table_time, table_x, table_y, table_r = tables
    rows_here, local_rcv, shot_count, sample_count = field_data.shape
    spectrum = jnp.einsum(
        "ckt,xryt->xckry",
        table_time,
        field_data.astype(jnp.bfloat16),
        preferred_element_type=jnp.float32,
    ).astype(jnp.bfloat16)
    bin_count = spectrum.shape[2]
    spectrum = spectrum.reshape(rows_here, 2, bin_count, local_rcv * shot_count)
    section_data = jnp.einsum(
        "akbx,xbfz->akfz",
        table_x,
        lax.all_to_all(spectrum, ("shot", "rep"), split_axis=2, concat_axis=0, tiled=True),
        preferred_element_type=jnp.float32,
    ).astype(jnp.bfloat16)
    all_rows, row_bins = (section_data.shape[1], section_data.shape[2])
    section_data = section_data.reshape(2, all_rows, row_bins, local_rcv, shot_count)
    section_data = lax.all_to_all(section_data, "rcv", split_axis=2, concat_axis=3, tiled=True)
    section_data = jnp.einsum(
        "ajby,bkfry->akfrj", table_y, section_data, preferred_element_type=jnp.float32
    ).astype(jnp.bfloat16)
    coefficients = jnp.einsum(
        "aqbr,bkfrj->akfqj", table_r, section_data, preferred_element_type=jnp.float32
    )
    shrunk = soft_limit(coefficients, threshold_row)
    section_data = jnp.einsum(
        "aqbr,akfqj->bkfrj", table_r, shrunk, preferred_element_type=jnp.float32
    ).astype(jnp.bfloat16)
    section_data = jnp.einsum(
        "ajby,akfrj->bkfry", table_y, section_data, preferred_element_type=jnp.float32
    ).astype(jnp.bfloat16)
    section_data = lax.all_to_all(section_data, "rcv", split_axis=3, concat_axis=2, tiled=True)
    section_data = section_data.reshape(2, all_rows, row_bins, local_rcv * shot_count)
    section_data = jnp.einsum(
        "akbx,akfz->bxfz", table_x, section_data, preferred_element_type=jnp.float32
    ).astype(jnp.bfloat16)
    result = jnp.einsum(
        "ckt,cxkz->xzt",
        table_time,
        lax.all_to_all(section_data, ("shot", "rep"), split_axis=1, concat_axis=2, tiled=True),
        preferred_element_type=jnp.float32,
    )
    return result.reshape(rows_here, local_rcv, shot_count, sample_count)


def body_by_rows(records, offsets, filter_index, signatures, thresholds):
    rows_here, shot_count = offsets.shape
    local_rcv, slab_len = records.shape
    slab_count = lax.axis_size(("shot", "rep"))
    rcv_count = lax.axis_size("rcv")
    tap_count = signatures.shape[1]
    sample_count = NT
    slab_blocks = slab_len // tap_count
    trace_blocks = sample_count // tap_count
    capacity = max(2, 2 * shot_count // slab_count)
    slot_count = slab_count * rows_here * capacity
    forward_tables = toeplitz_table(signatures, False)
    adjoint_tables = toeplitz_table(signatures, True)
    flat_index = filter_index.reshape(-1)
    forward_table = forward_tables[flat_index]
    adjoint_table = adjoint_tables[flat_index]
    owners = offsets // slab_len
    row_ids = jnp.arange(rows_here, dtype=jnp.int32)[:, None]
    slot_index = (
        owners * (rows_here * capacity) + row_ids * capacity + rank_in_row(owners)
    ).reshape(-1)
    every_offset = lax.all_gather(offsets, ("shot", "rep"), axis=0, tiled=True)
    every_owner = every_offset // slab_len
    every_start = every_offset // tap_count % slab_blocks
    every_rank = rank_in_row(every_owner)
    mine_mask = every_owner == lax.axis_index(("shot", "rep"))
    levels = jnp.arange(capacity, dtype=jnp.int32)
    picked = mine_mask[:, :, None] & (every_rank[:, :, None] == levels[None, None, :])
    table_in = jnp.sum(jnp.where(picked, every_start[:, :, None] + 1, 0), axis=1).reshape(-1)
    filled = table_in > 0
    block_steps = jnp.arange(trace_blocks, dtype=jnp.int32)
    target = jnp.where(
        filled[:, None],
        table_in[:, None] - 1 + block_steps[None, :],
        slab_blocks + trace_blocks - 1,
    )

    def correlate(record_field):
        record_low = (
            record_field.astype(jnp.bfloat16)
            .reshape(local_rcv, slab_blocks, tap_count)
            .transpose(1, 0, 2)
        )
        rim_blocks = from_behind(record_low[: trace_blocks - 1], ("shot", "rep"), -1)
        extended = jnp.concatenate(
            [record_low, rim_blocks, jnp.zeros((1, local_rcv, tap_count), jnp.bfloat16)], axis=0
        )
        windows = extended[target.reshape(-1)].reshape(
            slot_count, trace_blocks, local_rcv, tap_count
        )
        returned = to_shots(windows)
        traces = returned[slot_index]
        terms = apply_filter(traces, adjoint_table, True)
        terms = terms.reshape(rows_here, shot_count, trace_blocks, local_rcv, tap_count).transpose(
            0, 3, 1, 2, 4
        )
        return terms.reshape(rows_here, local_rcv, shot_count, sample_count)

    tables = (
        time_table(sample_count),
        shot_table(slab_count * rows_here),
        shot_table(shot_count),
        shot_table(local_rcv * rcv_count),
    )
    row_bins = sample_count // 2 // slab_count
    rcv_bins = row_bins // rcv_count
    bin_start = lax.axis_index(("shot", "rep")) * row_bins + lax.axis_index("rcv") * rcv_bins

    def threshold_for(level_index):
        return lax.dynamic_slice_in_dim(thresholds[level_index], bin_start, rcv_bins)

    model_field = shrink(correlate(records), threshold_for(0), tables)
    level_index = 1
    traces = model_field.astype(jnp.bfloat16).reshape(
        rows_here, local_rcv, shot_count, trace_blocks, tap_count
    )
    traces = traces.transpose(0, 2, 3, 1, 4).reshape(
        rows_here * shot_count, trace_blocks, local_rcv, tap_count
    )
    shots = apply_filter(traces, forward_table, False).astype(jnp.bfloat16)
    outgoing = (
        jnp.zeros((slot_count, trace_blocks, local_rcv, tap_count), jnp.bfloat16)
        .at[slot_index]
        .set(shots)
    )
    arrived = to_slabs(outgoing)
    slab_total = jnp.zeros((slab_blocks + trace_blocks, local_rcv, tap_count), jnp.float32)
    for block_step in range(trace_blocks):
        slab_total = slab_total.at[target[:, block_step]].add(
            arrived[:, block_step].astype(jnp.float32)
        )
    spill_over = slab_total[slab_blocks : slab_blocks + trace_blocks - 1]
    carried = from_behind(spill_over, ("shot", "rep"), 1)
    blended = slab_total[:slab_blocks].at[: trace_blocks - 1].add(carried)
    residual = records - blended.transpose(1, 0, 2).reshape(local_rcv, slab_len)
    model_field = shrink(model_field + correlate(residual), threshold_for(level_index), tables)
    return (model_field, residual)


def dot(left, right, left_dim=1, right_dim=0):
    return lax.dot_general(
        left, right, (((left_dim,), (right_dim,)), ((), ())), preferred_element_type=jnp.float32
    )


def fixed_time_table(count):
    samples = np.arange(count)
    bins = np.arange(count // 2)[:, None]
    angles = 2.0 * np.pi / count * (bins * samples[None, :] % count)
    scale = math.sqrt(2.0 / count)
    cosine = scale * np.cos(angles)
    sine = -scale * np.sin(angles)
    cosine[0] = math.sqrt(1.0 / count)
    sine[0] = math.sqrt(1.0 / count) * np.where(samples % 2 == 0, 1.0, -1.0)
    return np.stack([cosine, sine]).astype(jnp.bfloat16)


def fixed_shot_table(count):
    positions = np.arange(count)
    angles = 2.0 * np.pi / count * (positions[:, None] * positions[None, :] % count)
    cosine = np.cos(angles) / math.sqrt(count)
    sine = np.sin(angles) / math.sqrt(count)
    table = np.stack([np.stack([cosine, sine], 1), np.stack([-sine, cosine], 1)])
    return table.astype(jnp.bfloat16).astype(np.float32)


def analyse(with_model, starts_ref, picks_ref, blocks_ref, taps_ref, table_ref, *rest):
    model_ref = rest[0] if with_model else None
    out_ref, held_ref = rest[-2:]
    rcv, taps = blocks_ref.shape[1:]
    parts, _, bins, lanes = out_ref.shape
    slots = lanes // 2
    rows = held_ref.shape[0] // slots
    steps = rows // rcv
    half = parts * bins

    def one(slot, carry):
        window = blocks_ref[pl.ds(starts_ref[slot], steps)].reshape(rows, taps)
        later = jnp.concatenate([window[rcv:], jnp.zeros((rcv, taps), window.dtype)], axis=0)
        pair = jnp.concatenate([window, later], axis=1)
        terms = dot(pair, taps_ref[picks_ref[slot]])
        where = pl.ds(pl.multiple_of(slot * rows, rows), rows)
        if with_model:
            terms = terms + model_ref[where]
        held_ref[where] = terms
        return carry

    lax.fori_loop(0, slots, one, 0, unroll=8)
    together = math.gcd(rcv, 4)
    for first in range(0, rcv, together):
        traces = jnp.concatenate(
            [
                jnp.concatenate(
                    [
                        held_ref[pl.ds(step * rcv + line, slots, stride=rows), :].astype(jnp.bfloat16)
                        for step in range(steps)
                    ],
                    axis=1,
                )
                for line in range(first, first + together)
            ],
            axis=0,
        )
        both = dot(table_ref[...], traces, 1, 1)
        for line in range(together):
            piece = both[:, line * slots : (line + 1) * slots]
            joined = jnp.concatenate([piece[:half], piece[half:]], axis=1)
            out_ref[:, first + line] = joined.reshape(parts, bins, lanes).astype(jnp.bfloat16)


def slots_to_spectra(starts, picks, blocks, taps, table, model, parts, slots):
    rcv, width = blocks.shape[1:]
    samples = table.shape[1]
    vmem = pl.BlockSpec(memory_space=pltpu.VMEM)
    smem = pl.BlockSpec(memory_space=pltpu.SMEM)
    extra = () if model is None else (model,)
    return pl.pallas_call(
        functools.partial(analyse, model is not None),
        out_shape=jax.ShapeDtypeStruct((parts, rcv, samples // 2 // parts, 2 * slots), jnp.bfloat16),
        in_specs=[smem, smem, vmem, vmem, vmem] + [vmem] * len(extra),
        out_specs=vmem,
        scratch_shapes=[pltpu.VMEM((slots * rcv * samples // width, width), jnp.float32)],
    )(starts, picks, blocks, taps, table, *extra)


def upright(spectra_ref, lines, group_lanes):
    parts, _, bins, _ = spectra_ref.shape
    pieces = []
    for line in lines:
        turned = spectra_ref[:, line].reshape(parts * bins, -1).astype(jnp.float32).T
        turned = turned.astype(jnp.bfloat16)
        count = group_lanes // 2
        for low in range(0, turned.shape[0], group_lanes):
            pieces.append(
                jnp.concatenate(
                    [turned[low : low + count], turned[low + count : low + 2 * count]], axis=1
                )
            )
    return jnp.concatenate(pieces, axis=0)


def synthesise(starts_ref, picks_ref, spectra_ref, taps_ref, table_ref, model_ref, total_ref):
    rcv, lanes = spectra_ref.shape[1], spectra_ref.shape[3]
    slots = lanes // 2
    taps = model_ref.shape[1]
    rows = model_ref.shape[0] // slots
    steps = rows // rcv
    together = math.gcd(rcv, 4)
    for first in range(0, rcv, together):
        lines = range(first, first + together)
        fields = dot(upright(spectra_ref, lines, lanes), table_ref[...])
        for line in lines:
            low = (line - first) * slots
            for step in range(steps):
                model_ref[pl.ds(step * rcv + line, slots, stride=rows), :] = fields[
                    low : low + slots, step * taps : (step + 1) * taps
                ]
    total_ref[...] = jnp.zeros_like(total_ref)

    def one(slot, carry):
        trace = model_ref[pl.ds(pl.multiple_of(slot * rows, rows), rows)].astype(jnp.bfloat16)
        earlier = jnp.concatenate([jnp.zeros((rcv, taps), trace.dtype), trace[:-rcv]], axis=0)
        pair = jnp.concatenate([trace, earlier], axis=1)
        shot = dot(pair, taps_ref[picks_ref[slot]]).astype(jnp.bfloat16).astype(jnp.float32)
        where = pl.ds(starts_ref[slot], steps)
        total_ref[where] = total_ref[where] + shot.reshape(steps, rcv, taps)
        return carry

    lax.fori_loop(0, slots, one, 0, unroll=8)


def spectra_to_slab(starts, picks, spectra, taps, table, slab_blocks):
    _, rcv, _, lanes = spectra.shape
    width = taps.shape[2]
    steps = table.shape[1] // width
    vmem = pl.BlockSpec(memory_space=pltpu.VMEM)
    smem = pl.BlockSpec(memory_space=pltpu.SMEM)
    return pl.pallas_call(
        synthesise,
        out_shape=(
            jax.ShapeDtypeStruct((lanes // 2 * rcv * steps, width), jnp.float32),
            jax.ShapeDtypeStruct((slab_blocks + steps, rcv, width), jnp.float32),
        ),
        in_specs=[smem, smem, vmem, vmem, vmem],
        out_specs=(vmem, vmem),
    )(starts, picks, spectra, taps, table)


def record_kernel(groups, spectra_ref, table_ref, out_ref):
    count = out_ref.shape[2]
    together = spectra_ref.shape[1]
    fields = dot(upright(spectra_ref, range(together), 2 * count), table_ref[...])
    for line in range(together):
        for group in range(groups):
            low = (line * groups + group) * count
            out_ref[group, line] = fields[low : low + count]


def records_of(spectra, table, groups):
    parts, rcv, bins, lanes = spectra.shape
    samples = table.shape[1]
    count = lanes // 2 // groups
    together = math.gcd(rcv, 4)
    return pl.pallas_call(
        functools.partial(record_kernel, groups),
        grid=(rcv // together,),
        out_shape=jax.ShapeDtypeStruct((groups, rcv, count, samples), jnp.float32),
        in_specs=[
            pl.BlockSpec((parts, together, bins, lanes), lambda i: (0, i, 0, 0)),
            pl.BlockSpec((samples, samples), lambda i: (0, 0)),
        ],
        out_specs=pl.BlockSpec((groups, together, count, samples), lambda i: (0, i, 0, 0)),
    )(spectra, table)


def bins_kernel(place, halves, spectra_ref, go_ref, back_ref, cosine_ref, sine_ref, level_ref, out_ref):
    _, rcv, bins, lanes = spectra_ref.shape
    rows = rcv * bins
    rcv_count, slab_count = place.shape
    joined = jnp.concatenate(
        [
            jnp.concatenate(
                [spectra_ref[int(index)].reshape(rows, lanes) for index in line], axis=1
            )
            for line in place
        ],
        axis=0,
    )
    section = dot(joined, go_ref[...]).astype(jnp.bfloat16)
    half = section.shape[1] // 2
    near = dot(cosine_ref[...], section)
    far = dot(sine_ref[...], section)
    real = near[:, :half] + far[:, half:]
    imag = near[:, half:] - far[:, :half]
    level = level_ref[...]
    factor = 1.0 - level / jnp.maximum(jnp.sqrt(real * real + imag * imag), level)
    shrunk = jnp.concatenate([real * factor, imag * factor], axis=1).astype(jnp.bfloat16)
    near = dot(cosine_ref[...], shrunk)
    far = dot(sine_ref[...], shrunk)
    section = jnp.concatenate(
        [near[:, :half] - far[:, half:], far[:, :half] + near[:, half:]], axis=1
    ).astype(jnp.bfloat16)
    result = dot(section, back_ref[...], 1, 1).astype(jnp.bfloat16)
    width = result.shape[1] // slab_count
    for line in range(rcv_count):
        for slab in range(slab_count):
            piece = result[line * rows : (line + 1) * rows, slab * width : (slab + 1) * width]
            if halves == 2:
                piece = jnp.concatenate([piece[: rows // 2], piece[rows // 2 :]], axis=1)
            out_ref[int(place[line, slab])] = piece.reshape(rcv // halves, bins, halves * width)


def bins_stage(spectra, go, back, cosine, sine, level, place, halves):
    parts, rcv, bins, _ = spectra.shape
    width = halves * back.shape[0] // place.shape[1]
    vmem = pl.BlockSpec(memory_space=pltpu.VMEM)
    return pl.pallas_call(
        functools.partial(bins_kernel, place, halves),
        out_shape=jax.ShapeDtypeStruct((parts, rcv // halves, bins, width), jnp.bfloat16),
        in_specs=[vmem] * 6,
        out_specs=vmem,
    )(spectra, go, back, cosine, sine, level)


def body_by_slots(records, offsets, filter_index, signatures, thresholds):
    rows_here, shot_count = offsets.shape
    local_rcv, slab_len = records.shape
    slab_count = lax.axis_size(("shot", "rep"))
    rep_count = lax.axis_size("rep")
    rcv_count = lax.axis_size("rcv")
    parts = slab_count * rcv_count
    everyone = ("shot", "rcv", "rep")
    tap_count = signatures.shape[1]
    slab_blocks = slab_len // tap_count
    steps = NT // tap_count
    capacity = max(2, 2 * shot_count // slab_count)
    row_count = rows_here * slab_count
    slots = row_count * capacity
    bins = NT // 2 // parts
    place = np.array(
        [
            [((slab // rep_count) * rcv_count + line) * rep_count + slab % rep_count for slab in range(slab_count)]
            for line in range(rcv_count)
        ]
    )

    time_table_fixed = jnp.asarray(fixed_time_table(NT).reshape(NT, NT))
    table_x, table_y, table_r = (
        fixed_shot_table(count) for count in (row_count, shot_count, local_rcv * rcv_count)
    )
    grid_table = np.einsum("ajby,bkcx->cxyakj", table_y, table_x).astype(jnp.bfloat16)
    row_table = np.ascontiguousarray(grid_table.transpose(1, 0, 2, 3, 4, 5))
    points = 2 * row_count * shot_count
    grid_table = jnp.asarray(grid_table.reshape(points, points))
    row_table = jnp.asarray(row_table.reshape(points, points))
    same = np.eye(bins, dtype=np.float32)
    cosine = jnp.asarray(np.kron(table_r[0, :, 0], same).astype(jnp.bfloat16))
    sine = jnp.asarray(np.kron(table_r[0, :, 1], same).astype(jnp.bfloat16))

    shots = jnp.stack([offsets, filter_index])
    every = lax.all_to_all(
        jnp.broadcast_to(shots[None], (slab_count,) + shots.shape), ("shot", "rep"), 0, 0, tiled=True
    )
    every_offset = every[:, 0].reshape(row_count, shot_count)
    every_pick = every[:, 1].reshape(row_count, shot_count)
    every_owner = every_offset // slab_len
    every_rank = rank_in_row(every_owner)
    slabs = jnp.arange(slab_count, dtype=jnp.int32)
    ranks = jnp.arange(capacity, dtype=jnp.int32)
    taken = (every_owner[None, :, None, :] == slabs[:, None, None, None]) & (
        every_rank[None, :, None, :] == ranks[None, None, :, None]
    )
    point_of = jnp.arange(row_count * shot_count, dtype=jnp.int32).reshape(row_count, shot_count)
    code = jnp.sum(jnp.where(taken, point_of[None, :, None, :] + 1, 0), axis=3).reshape(
        slab_count, 1, slots
    )
    code = jnp.where(
        code > 0, code - 1 + row_count * shot_count * jnp.arange(2, dtype=jnp.int32)[None, :, None], -1
    ).reshape(-1)
    chosen = (code[:, None] == jnp.arange(points, dtype=jnp.int32)[None, :]).astype(jnp.bfloat16)
    slot_table = dot(chosen, grid_table).astype(jnp.bfloat16)
    mine = (every_owner == lax.axis_index(("shot", "rep")))[:, None, :] & (
        every_rank[:, None, :] == ranks[None, :, None]
    )
    every_start = every_offset // tap_count % slab_blocks
    starts = jnp.sum(jnp.where(mine, every_start[:, None, :], 0), axis=2).reshape(-1)
    picks = jnp.sum(jnp.where(mine, every_pick[:, None, :], 0), axis=2).reshape(-1)
    adjoint_tables = toeplitz_table(signatures, True)

    def correlate(blocks, rim, model):
        low = blocks.astype(jnp.bfloat16)
        extended = jnp.concatenate([low, rim, jnp.zeros_like(low[:1])], axis=0)
        return slots_to_spectra(
            starts, picks, extended, adjoint_tables, time_table_fixed, model, parts, slots
        )

    bin_start = lax.axis_index(everyone) * bins

    def swap(value):
        return lax.all_to_all(value, everyone, 0, 0, tiled=True)

    def shrink_at(spectra, index, back, halves):
        level = lax.dynamic_slice_in_dim(thresholds[index], bin_start, bins)
        level = jnp.tile(level, local_rcv * rcv_count)[:, None]
        return bins_stage(swap(spectra), slot_table, back, cosine, sine, level, place, halves)

    record_blocks = records.reshape(local_rcv, slab_blocks, tap_count).transpose(1, 0, 2)
    rim = from_behind(record_blocks[: steps - 1].astype(jnp.bfloat16), ("shot", "rep"), -1)
    spectra = shrink_at(correlate(record_blocks, rim, None), 0, slot_table, 1)
    spectra, taps = lax.optimization_barrier((spectra, signatures))
    forward_tables = toeplitz_table(taps, False)
    model, total = spectra_to_slab(
        starts, picks, swap(spectra), forward_tables, time_table_fixed, slab_blocks
    )
    spill = total[slab_blocks : slab_blocks + steps - 1]
    left = record_blocks - total[:slab_blocks]
    carried = from_behind(spill, ("shot", "rep"), 1)
    ahead = from_behind(left[: steps - 1], ("shot", "rep"), -1)
    left = left.at[: steps - 1].add(-carried)
    rim = (ahead - spill).astype(jnp.bfloat16)
    residual = left.transpose(1, 0, 2).reshape(local_rcv, slab_len)
    spectra = swap(shrink_at(correlate(left, rim, model), 1, row_table, 2))
    model = records_of(spectra, time_table_fixed, 2)
    return (model.reshape(rows_here, local_rcv, shot_count, NT), residual)


def body(records, offsets, filter_index, signatures, thresholds):
    rows_here, shot_count = offsets.shape
    slab_count = lax.axis_size(("shot", "rep"))
    parts = slab_count * lax.axis_size("rcv")
    slots = rows_here * slab_count * max(2, 2 * shot_count // slab_count)
    table_rows = 2 * rows_here * slab_count * shot_count
    fits = table_rows <= 1024 and rows_here == 1 and slots == 64 and 4 * shot_count == 128
    fits = fits and records.shape[0] == 16 and NT // 2 // parts == 16
    run = body_by_slots if fits else body_by_rows
    return run(records, offsets, filter_index, signatures, thresholds)


def solution(mesh):
    in_specs = (
        P(("groups", "rcv"), ("shot", "rep")),
        P(("groups", "shot", "rep"), None),
        P(("groups", "shot", "rep"), None),
        P(),
        P(),
    )
    out_specs = (
        P(("groups", "shot", "rep"), "rcv", None, None),
        P(("groups", "rcv"), ("shot", "rep")),
    )
    return jax.shard_map(body, mesh=mesh, in_specs=in_specs, out_specs=out_specs, check_vma=False)
```
